32 devices in a mesh: lines: 2 (over y), shots: 16 (over z, x, core).
Axes of the slice: x: 2, y: 2, z: 4, core: 2. Of those that a mesh axis runs over, the one named last changes fastest.
Arguments:
- records: bfloat16 [2048, 1024, 256], P(('lines', 'shots')), parts along dimension 0, may hold values from -6 to 6
- missing: int32 [256], P('lines'), parts along dimension 0, may hold values from 0 to 1023, as said below
- neighbours: int32 [256, 3], P('lines'), parts along dimension 0, may hold values from 0 to 1023, as said below
- weights: float32 [256, 3], P('lines'), parts along dimension 0, may hold values from 0.2 to 0.6
- freq_bins: int32 [8], replicated, may hold values from 1 to 127, as said below
Outputs:
- multiples: bfloat16 [2048, 1024, 256], P(('lines', 'shots')), parts along dimension 0
The draws below stay inside these ranges and needn't reach their ends.
There are 2 independent parts, one for each index of `lines`. The reference program is written for one: setup_inputs(seed, part) draws one part's arguments, and reference() takes and returns one part's arrays. A program takes and returns all parts, laid end to end along the dimension named above; an argument that names none is the same for every part. Nothing has to cross between parts.
Inputs may be any that keep to these rules, and one draw needn't show every extreme that they name: `missing`: distinct and ascending; any two missing shots lie 3 or more apart, and every shot within 2 of a missing shot is recorded. `neighbours`: row i names 3 distinct recorded shots, each within 2 of missing[i]. `freq_bins`: 8 distinct bins.
All inputs are finite; a program needn't handle non-finite values.
Results may differ from the reference program's by a relative error of at most 0.0079.
Values may be sent and summed in bfloat16 or wider, within the bound.
No kernel may reach another device: no remote copies, remote signals or barrier semaphores. Data moves between devices by JAX's collectives and lax.ppermute only.
A program may use at most 192 MiB of HBM per device.

```python
import math
import jax
import jax.numpy as jnp
from jax import lax

SHOTS = 1024
SAMPLES = 256
REACH = 2
NEIGH = 3
NMISS = 128
NFREQ = 8


def missing_layout(key):
    slot_count = SHOTS // 4
    slot_order = jax.random.permutation(jax.random.fold_in(key, 101), slot_count - 2)[:NMISS] + 1
    chosen = jnp.sort(slot_order)
    offset = jax.random.randint(jax.random.fold_in(key, 102), (NMISS,), 2, 4)
    return (chosen * 4 + offset).astype(jnp.int32)


def draw_missing(key, part):
    return missing_layout(key)


def draw_neighbours(key, part):
    missing = missing_layout(key)
    offsets = jnp.concatenate([-jnp.arange(1, REACH + 1), jnp.arange(1, REACH + 1)]).astype(jnp.int32)
    scores = jax.random.randint(jax.random.fold_in(key, 103), (NMISS, 2 * REACH), 0, 4096) * (2 * REACH) + jnp.arange(2 * REACH)[None, :]
    picked = jnp.argsort(scores, axis=1)[:, :NEIGH]
    return (missing[:, None] + offsets[picked]).astype(jnp.int32)


def draw_freq_bins(key, part):
    middle = jax.random.permutation(jax.random.fold_in(key, 201), SAMPLES // 2 - 3)[:NFREQ - 2] + 2
    complete = jnp.concatenate([middle, jnp.array([1, SAMPLES // 2 - 1])])
    shuffle = jax.random.permutation(jax.random.fold_in(key, 202), NFREQ)
    return complete[shuffle].astype(jnp.int32)


def steps_of(own_key, dims, cuts, low, largest):
    factor_of, own = 1.0, jax.random.fold_in(own_key, 6)
    for dim, parts in cuts:
        heights = jnp.exp(jax.random.uniform(jax.random.fold_in(own, dim), (parts,), jnp.float32, low / len(cuts), largest / len(cuts)))
        factor_of = factor_of * jnp.repeat(heights, dims[dim] // parts).reshape([-1 if axis == dim else 1 for axis in range(len(dims))])
    return factor_of


def normal_values(key, extent, spread, reach, pieces=(), kind=jnp.bfloat16):
    values = spread * jax.random.normal(key, extent, jnp.float32)
    if pieces:
        values = values * steps_of(key, extent, pieces, -0.22, 0.18)
    return jnp.clip(values, -reach, reach).astype(kind)


def setup_inputs(seed: int = 0, part: int = 0) -> dict:
    arg_keys = jax.random.split(jax.random.key(seed), 6)
    part_keys = jax.random.split(jax.random.fold_in(arg_keys[5], part), 6)
    return {
        "records": normal_values(part_keys[0], (SHOTS, SHOTS, SAMPLES), 1.0, 6.0, ((0, 16),)),
        "missing": draw_missing(jax.random.fold_in(jax.random.fold_in(arg_keys[5], part), 71), part),
        "neighbours": draw_neighbours(jax.random.fold_in(jax.random.fold_in(arg_keys[5], part), 71), part),
        "weights": jnp.clip(jax.random.uniform(part_keys[3], (NMISS, NEIGH), jnp.float32, 0.2, 0.6), 0.2, 0.6),
        "freq_bins": draw_freq_bins(jax.random.fold_in(arg_keys[5], 71), part),
    }


def tables(freq_bins):
    sample_ids = jnp.arange(SAMPLES, dtype=jnp.int32)
    phases = freq_bins[None, :] * sample_ids[:, None] % SAMPLES
    angles = phases.astype(jnp.float32) * (2.0 * math.pi / SAMPLES)
    trig_pair = jnp.stack([jnp.cos(angles), -jnp.sin(angles)], axis=-1)
    forward = (trig_pair / math.sqrt(SAMPLES)).astype(jnp.bfloat16)
    inverse = (trig_pair * math.sqrt(2.0 / NFREQ)).astype(jnp.bfloat16)
    return (forward, inverse)

def product_plane(plane_pair):
    real_part = plane_pair[0].astype(jnp.float32)
    imag_part = plane_pair[1].astype(jnp.float32)
    left_side = jnp.concatenate([real_part, imag_part], axis=1)
    right_side = jnp.concatenate([jnp.concatenate([real_part, imag_part], axis=1), jnp.concatenate([-imag_part, real_part], axis=1)], axis=0)
    factor = -1.0 / math.sqrt(SHOTS)
    summed = jnp.dot(left_side, right_side, precision=lax.Precision.HIGHEST)
    return (summed * factor).astype(jnp.bfloat16)

def reference(records, missing, neighbours, weights, freq_bins):
    forward, inverse = tables(freq_bins)
    spectra = jnp.dot(records.reshape(SHOTS * SHOTS, SAMPLES), forward.reshape(SAMPLES, 2 * NFREQ), preferred_element_type=jnp.float32)
    spectra = spectra.astype(jnp.bfloat16).reshape(SHOTS, SHOTS, NFREQ, 2)
    filled_rows = jnp.zeros((NMISS, SHOTS, NFREQ, 2), jnp.float32)
    for slot_index in range(NEIGH):
        picked = spectra[neighbours[:, slot_index]].astype(jnp.float32)
        filled_rows = filled_rows + weights[:, slot_index][:, None, None, None] * picked
    filled = spectra.at[missing].set(filled_rows.astype(jnp.bfloat16))
    planes = jnp.transpose(filled, (2, 3, 0, 1))
    predicted = lax.map(product_plane, planes)
    stacked = jnp.transpose(predicted.reshape(NFREQ, SHOTS, 2, SHOTS), (1, 3, 0, 2))
    inverse_rows = jnp.transpose(inverse, (1, 2, 0)).reshape(2 * NFREQ, SAMPLES)
    multiples = jnp.dot(stacked.reshape(SHOTS * SHOTS, 2 * NFREQ), inverse_rows, preferred_element_type=jnp.float32)
    return multiples.astype(jnp.bfloat16).reshape(SHOTS, SHOTS, SAMPLES)
```

```python
import functools
import math

import jax
import jax.numpy as jnp
from jax import lax
from jax.experimental import pallas as pl
from jax.experimental.pallas import tpu as pltpu
from jax.sharding import PartitionSpec as P

CHUNKS = 4
LANES = 128
VMEM_LIMIT = 48 * 1024 * 1024


def tables(freq_bins, sample_count):
    bin_count = freq_bins.shape[0]
    sample_ids = jnp.arange(sample_count, dtype=jnp.int32)
    phases = freq_bins[None, :] * sample_ids[:, None] % sample_count
    angles = phases.astype(jnp.float32) * (2.0 * math.pi / sample_count)
    trig_pair = jnp.stack([jnp.cos(angles), -jnp.sin(angles)], axis=-1)
    forward = (trig_pair / math.sqrt(sample_count)).astype(jnp.bfloat16)
    inverse = (trig_pair * math.sqrt(2.0 / bin_count)).astype(jnp.bfloat16)
    rows = lambda table: jnp.transpose(table, (1, 2, 0)).reshape(2 * bin_count, sample_count)
    return rows(forward), rows(inverse)


def shot_step(shot_rows):
    return math.gcd(shot_rows, 16)


def forward_body(records_ref, table_ref, out_ref, rows_ref):
    steps, halves, width, samples = records_ref.shape
    planes = table_ref.shape[0]
    flat = records_ref[...].reshape(steps * halves * width, samples)
    spectra = lax.dot_general(
        table_ref[...], flat, (((1,), (1,)), ((), ())), preferred_element_type=jnp.float32
    )
    for shot in range(steps):
        for half in range(halves):
            start = (shot * halves + half) * width
            rows_ref[half, :, shot, :] = spectra[:, start : start + width]
    for half in range(halves):
        out_ref[:, half] = (
            rows_ref[half].astype(jnp.bfloat16).reshape(planes // 2, 2, steps, width)
        )


def forward_chunk(records, table, chunk, width):
    shot_rows, halves, half, samples = records.shape
    planes = table.shape[0]
    step = shot_step(shot_rows)
    bins = planes // 2
    return pl.pallas_call(
        forward_body,
        grid=(shot_rows // step,),
        in_specs=[
            pl.BlockSpec((step, halves, width, samples), lambda i: (i, 0, chunk, 0)),
            pl.BlockSpec((planes, samples), lambda i: (0, 0)),
        ],
        out_specs=pl.BlockSpec((bins, halves, 2, step, width), lambda i: (0, 0, 0, i, 0)),
        out_shape=jax.ShapeDtypeStruct((bins, halves, 2, shot_rows, width), jnp.bfloat16),
        scratch_shapes=[pltpu.VMEM((halves, planes, step, width), jnp.float32)],
        compiler_params=pltpu.CompilerParams(vmem_limit_bytes=VMEM_LIMIT),
        cost_estimate=pl.CostEstimate(
            flops=2 * shot_rows * halves * width * samples * planes,
            bytes_accessed=2 * shot_rows * halves * width * samples,
            transcendentals=0,
        ),
        name=f"forward_{chunk}",
    )(records, table)


def inverse_body(planes_ref, table_ref, kept_ref, out_ref, rows_ref):
    bins, halves, parts, steps, width = planes_ref.shape
    planes = bins * parts
    samples = table_ref.shape[1]
    for half in range(halves):
        rows_ref[half] = (
            planes_ref[:, half].astype(jnp.float32).reshape(planes, steps, width)
        )
    for shot in range(steps):
        for half in range(halves):
            left = rows_ref[half, :, shot, :].astype(jnp.bfloat16)
            out_ref[shot, half] = lax.dot_general(
                left, table_ref[...], (((0,), (0,)), ((), ())), preferred_element_type=jnp.float32
            ).astype(jnp.bfloat16)


def inverse_first(planes_ref, table_ref, out_ref, rows_ref):
    inverse_body(planes_ref, table_ref, None, out_ref, rows_ref)


def inverse_chunk(returned, table, kept, chunk, half):
    bins, halves, parts, shot_rows, width = returned.shape
    planes, samples = table.shape
    step = shot_step(shot_rows)
    in_specs = [
        pl.BlockSpec((bins, halves, parts, step, width), lambda i: (0, 0, 0, i, 0)),
        pl.BlockSpec((planes, samples), lambda i: (0, 0)),
    ]
    operands = [returned, table]
    if kept is not None:
        in_specs.append(pl.BlockSpec(memory_space=pl.ANY))
        operands.append(kept)
    return pl.pallas_call(
        inverse_first if kept is None else inverse_body,
        grid=(shot_rows // step,),
        in_specs=in_specs,
        out_specs=pl.BlockSpec((step, halves, width, samples), lambda i: (i, 0, chunk, 0)),
        out_shape=jax.ShapeDtypeStruct((shot_rows, halves, half, samples), jnp.bfloat16),
        scratch_shapes=[pltpu.VMEM((halves, planes, step, width), jnp.float32)],
        input_output_aliases={} if kept is None else {2: 0},
        compiler_params=pltpu.CompilerParams(vmem_limit_bytes=VMEM_LIMIT),
        cost_estimate=pl.CostEstimate(
            flops=2 * shot_rows * halves * width * samples * planes,
            bytes_accessed=2 * shot_rows * halves * width * samples,
            transcendentals=0,
        ),
        name=f"inverse_{chunk}",
    )(*operands)


def fill_body(spectra_ref, pick_ref, place_ref, keep_ref, out_ref):
    devices, parts, rows, width = spectra_ref.shape
    count = pick_ref.shape[0] // 2
    for part in range(parts):
        recorded = spectra_ref[:, part].reshape(devices * rows, width)
        both = jnp.dot(pick_ref[...], recorded, preferred_element_type=jnp.float32)
        replaced = (both[:count] + both[count:]).astype(jnp.bfloat16)
        placed = jnp.dot(place_ref[...], replaced, preferred_element_type=jnp.float32)
        kept = recorded.astype(jnp.float32) * keep_ref[...]
        out_ref[part] = (placed + kept).astype(jnp.bfloat16)


def fill(spectra, pick, place, keep):
    devices, parts, rows, width = spectra.shape
    order = devices * rows
    return pl.pallas_call(
        fill_body,
        out_shape=jax.ShapeDtypeStruct((parts, order, width), jnp.bfloat16),
        compiler_params=pltpu.CompilerParams(vmem_limit_bytes=VMEM_LIMIT),
        cost_estimate=pl.CostEstimate(
            flops=8 * pick.shape[0] * order * width,
            bytes_accessed=8 * order * width,
            transcendentals=0,
        ),
        name="fill",
    )(spectra, pick, place, keep)


def product_body(member_ref, *refs, chunks, scale):
    own_refs, other_refs = refs[:chunks], refs[chunks : 2 * chunks]
    right_ref, out_ref = refs[2 * chunks], refs[2 * chunks + 1]
    devices, parts, rows, width = out_ref.shape
    order = devices * rows
    half = chunks * width
    member = member_ref[0]
    total = jnp.zeros((order, 2 * width), jnp.float32)
    for source, lefts in enumerate((own_refs, other_refs)):
        first = (member if source == 0 else 1 - member) * half
        for index in range(chunks):
            start = pl.multiple_of(first + index * width, width)
            real = right_ref[0, pl.ds(start, width), :]
            imag = right_ref[1, pl.ds(start, width), :]
            left = lefts[index]
            total += jnp.dot(
                left[0], jnp.concatenate([real, imag], axis=1), preferred_element_type=jnp.float32
            )
            total += jnp.dot(
                left[1], jnp.concatenate([-imag, real], axis=1), preferred_element_type=jnp.float32
            )
    total = total * scale
    for part in range(parts):
        out_ref[:, part] = (
            total[:, part * width : (part + 1) * width]
            .astype(jnp.bfloat16)
            .reshape(devices, rows, width)
        )


def product(member, own, other, chunk, devices):
    chunks = len(own)
    parts, order, width = own[0].shape
    scale = -1.0 / math.sqrt(order)
    vmem = pl.BlockSpec(memory_space=pltpu.VMEM)
    return pl.pallas_call(
        functools.partial(product_body, chunks=chunks, scale=scale),
        in_specs=[pl.BlockSpec(memory_space=pltpu.SMEM)] + [vmem] * (2 * chunks + 1),
        out_specs=vmem,
        out_shape=jax.ShapeDtypeStruct((devices, parts, order // devices, width), jnp.bfloat16),
        compiler_params=pltpu.CompilerParams(vmem_limit_bytes=VMEM_LIMIT),
        cost_estimate=pl.CostEstimate(
            flops=16 * order * order * width, bytes_accessed=8 * order * order, transcendentals=0
        ),
        name=f"product_{chunk}",
    )(member, *own, *other, own[chunk])


def fill_tables(missing, neighbours, weights, order):
    shots = jnp.arange(order, dtype=jnp.int32)
    pick = jnp.zeros((missing.shape[0], order), jnp.float32)
    for slot in range(neighbours.shape[1]):
        pick = pick + jnp.where(
            neighbours[:, slot][:, None] == shots[None, :], weights[:, slot][:, None], 0.0
        )
    high = pick.astype(jnp.bfloat16)
    low = (pick - high.astype(jnp.float32)).astype(jnp.bfloat16)
    found = shots[:, None] == missing[None, :]
    keep = 1.0 - jnp.any(found, axis=1, keepdims=True).astype(jnp.float32)
    return jnp.concatenate([high, low], axis=0), found.astype(jnp.bfloat16), keep


def exchange(blocks):
    return lax.all_to_all(blocks, "shots", split_axis=0, concat_axis=0, tiled=True)


def shards(records, missing, neighbours, weights, freq_bins):
    devices = lax.axis_size("shots")
    position = lax.axis_index("shots")
    shot_rows, order, samples = records.shape
    half = order // 2
    chunks = CHUNKS
    width = half // chunks
    bins = freq_bins.shape[0]
    forward, inverse = tables(freq_bins, samples)
    pick, place, keep = fill_tables(missing, neighbours, weights, order)
    split = records.reshape(shot_rows, 2, half, samples)
    own = []
    for chunk in range(chunks):
        outgoing = forward_chunk(split, forward, chunk, width)
        incoming = exchange(outgoing.reshape(devices, 2, shot_rows, width))
        own.append(fill(incoming, pick, place, keep))
    pairs = [(i, i ^ 1) for i in range(devices)]
    other = [lax.ppermute(block, "shots", pairs) for block in own]
    member = (position % 2).astype(jnp.int32).reshape(1)
    result = None
    for chunk in range(chunks):
        predicted = product(member, own, other, chunk, devices)
        returned = exchange(predicted).reshape(bins, 2, 2, shot_rows, width)
        result = inverse_chunk(returned, inverse, result, chunk, half)
    return result.reshape(shot_rows, order, samples)


def solution(mesh):
    return jax.shard_map(
        shards,
        mesh=mesh,
        in_specs=(
            P(("lines", "shots"), None, None),
            P("lines"),
            P("lines", None),
            P("lines", None),
            P(),
        ),
        out_specs=P(("lines", "shots"), None, None),
        check_vma=False,
    )
```

```python
import functools
import math

import jax
import jax.numpy as jnp
from jax import lax
from jax.experimental import pallas as pl
from jax.experimental.pallas import tpu as pltpu
from jax.sharding import PartitionSpec as P


SHARES = (1, 2, 2, 2, 1)
STREAM_VMEM = 36 * 1024 * 1024
VMEM_LIMIT = 16 * 1024 * 1024


def tables(freq_bins, sample_count):
    bin_count = freq_bins.shape[0]
    sample_ids = jnp.arange(sample_count, dtype=jnp.int32)
    phases = freq_bins[None, :] * sample_ids[:, None] % sample_count
    angles = phases.astype(jnp.float32) * (2.0 * math.pi / sample_count)
    trig_pair = jnp.stack([jnp.cos(angles), -jnp.sin(angles)], axis=-1)
    forward = (trig_pair / math.sqrt(sample_count)).astype(jnp.bfloat16)
    inverse = (trig_pair * math.sqrt(2.0 / bin_count)).astype(jnp.bfloat16)
    rows = lambda table: jnp.transpose(table, (1, 2, 0)).reshape(2 * bin_count, sample_count)
    return rows(forward), rows(inverse)


def shot_step(shot_rows):
    return math.gcd(shot_rows, 16)


def forward_body(records_ref, table_ref, out_ref, rows_ref):
    steps, width, samples = records_ref.shape
    planes = table_ref.shape[0]
    flat = records_ref[...].reshape(steps * width, samples)
    spectra = lax.dot_general(
        table_ref[...], flat, (((1,), (1,)), ((), ())), preferred_element_type=jnp.float32
    )
    for shot in range(steps):
        rows_ref[:, shot, :] = spectra[:, shot * width : (shot + 1) * width]
    out_ref[...] = rows_ref[...].astype(jnp.bfloat16).reshape(planes // 2, 2, steps, width)


def forward_chunk(records, table, first, width):
    shot_rows, _, samples = records.shape
    planes = table.shape[0]
    step = shot_step(shot_rows)
    return pl.pallas_call(
        forward_body,
        grid=(shot_rows // step,),
        in_specs=[
            pl.BlockSpec(
                (pl.Element(step), pl.Element(width), pl.Element(samples)),
                lambda i: (i * step, first, 0),
            ),
            pl.BlockSpec((planes, samples), lambda i: (0, 0)),
        ],
        out_specs=pl.BlockSpec((planes // 2, 2, step, width), lambda i: (0, 0, i, 0)),
        out_shape=jax.ShapeDtypeStruct((planes // 2, 2, shot_rows, width), jnp.bfloat16),
        scratch_shapes=[pltpu.VMEM((planes, step, width), jnp.float32)],
        compiler_params=pltpu.CompilerParams(vmem_limit_bytes=STREAM_VMEM),
        cost_estimate=pl.CostEstimate(
            flops=2 * shot_rows * width * samples * planes,
            bytes_accessed=2 * shot_rows * width * samples,
            transcendentals=0,
        ),
    )(records, table)


def inverse_body(planes_ref, table_ref, *refs):
    out_ref, rows_ref = refs[-2:]
    bins, parts, steps, width = planes_ref.shape
    rows_ref[...] = planes_ref[...].astype(jnp.float32).reshape(bins * parts, steps, width)
    for shot in range(steps):
        left = rows_ref[:, shot, :].astype(jnp.bfloat16)
        out_ref[shot] = lax.dot_general(
            left, table_ref[...], (((0,), (0,)), ((), ())), preferred_element_type=jnp.float32
        ).astype(jnp.bfloat16)


def inverse_chunk(returned, table, kept, first, order):
    bins, parts, shot_rows, width = returned.shape
    planes, samples = table.shape
    step = shot_step(shot_rows)
    in_specs = [
        pl.BlockSpec((bins, parts, step, width), lambda i: (0, 0, i, 0)),
        pl.BlockSpec((planes, samples), lambda i: (0, 0)),
    ]
    operands = [returned, table]
    if kept is not None:
        in_specs.append(pl.BlockSpec(memory_space=pl.ANY))
        operands.append(kept)
    return pl.pallas_call(
        inverse_body,
        grid=(shot_rows // step,),
        in_specs=in_specs,
        out_specs=pl.BlockSpec(
            (pl.Element(step), pl.Element(width), pl.Element(samples)),
            lambda i: (i * step, first, 0),
        ),
        out_shape=jax.ShapeDtypeStruct((shot_rows, order, samples), jnp.bfloat16),
        scratch_shapes=[pltpu.VMEM((planes, step, width), jnp.float32)],
        input_output_aliases={} if kept is None else {2: 0},
        compiler_params=pltpu.CompilerParams(vmem_limit_bytes=STREAM_VMEM),
        cost_estimate=pl.CostEstimate(
            flops=2 * shot_rows * width * samples * planes,
            bytes_accessed=2 * shot_rows * width * samples,
            transcendentals=0,
        ),
    )(*operands)


def filled_rows(recorded, edge, pick, place, keep):
    count = pick.shape[0] // 2
    known = jnp.concatenate([recorded, edge], axis=0)
    both = jnp.dot(pick, known, preferred_element_type=jnp.float32)
    replaced = (both[:count] + both[count:]).astype(jnp.bfloat16)
    placed = jnp.dot(place, replaced, preferred_element_type=jnp.float32)
    return (placed + recorded.astype(jnp.float32) * keep).astype(jnp.bfloat16)


def fill_body(*refs, firsts):
    own_refs = refs[: len(firsts)]
    edge_ref, pick_ref, place_ref, keep_ref, out_ref = refs[len(firsts) :]
    order = edge_ref.shape[2]
    for own_ref, first in zip(own_refs, firsts):
        sources, parts, rows, width = own_ref.shape
        for part in range(parts):
            recorded = own_ref[:, part].reshape(sources * rows, width)
            edge = edge_ref[part, :, first : first + width]
            start = part * order + first
            out_ref[:, start : start + width] = filled_rows(
                recorded, edge, pick_ref[...], place_ref[...], keep_ref[...]
            )


def fill_own(own, edge, tables_own, firsts):
    sources, parts, rows, _ = own[0].shape
    order = edge.shape[2]
    return pl.pallas_call(
        functools.partial(fill_body, firsts=firsts),
        out_shape=jax.ShapeDtypeStruct((sources * rows, parts * order), jnp.bfloat16),
        compiler_params=pltpu.CompilerParams(vmem_limit_bytes=VMEM_LIMIT),
        cost_estimate=pl.CostEstimate(
            flops=8 * tables_own[0].shape[0] * sources * rows * order,
            bytes_accessed=8 * sources * rows * order,
            transcendentals=0,
        ),
        name="fill_own",
    )(*own, edge, *tables_own)


def product_body(
    side_ref, other_ref, edge_ref, pick_ref, place_ref, keep_ref, left_ref, out_ref, right_ref, *, first, scale
):
    sources, parts, rows, width = other_ref.shape
    half = sources * rows
    order = left_ref.shape[1] // 2
    side = side_ref[0]
    other = [
        filled_rows(
            other_ref[:, part].reshape(half, width),
            edge_ref[part],
            pick_ref[...],
            place_ref[...],
            keep_ref[...],
        )
        for part in range(parts)
    ]
    own = [left_ref[:, part * order + first : part * order + first + width] for part in range(parts)]
    for real, imag, at in ((own[0], own[1], side), (other[0], other[1], 1 - side)):
        start = pl.multiple_of(at * half, half)
        right_ref[pl.ds(start, half), :width] = real
        right_ref[pl.ds(start, half), width:] = imag
        start = pl.multiple_of(at * half + order, half)
        right_ref[pl.ds(start, half), :width] = -imag
        right_ref[pl.ds(start, half), width:] = real
    total = jnp.dot(left_ref[...], right_ref[...], preferred_element_type=jnp.float32) * scale
    for part in range(parts):
        out_ref[:, part] = (
            total[:, part * width : (part + 1) * width]
            .astype(jnp.bfloat16)
            .reshape(sources, rows, width)
        )


def product(side, other, edge, tables_other, left, first):
    sources, parts, rows, width = other.shape
    half = sources * rows
    order = left.shape[1] // parts
    vmem = pl.BlockSpec(memory_space=pltpu.VMEM)
    return pl.pallas_call(
        functools.partial(product_body, first=first, scale=-1.0 / math.sqrt(order)),
        in_specs=[pl.BlockSpec(memory_space=pltpu.SMEM)] + [vmem] * 6,
        out_specs=vmem,
        out_shape=jax.ShapeDtypeStruct((sources, parts, rows, width), jnp.bfloat16),
        scratch_shapes=[pltpu.VMEM((2 * order, 2 * width), jnp.bfloat16)],
        compiler_params=pltpu.CompilerParams(vmem_limit_bytes=VMEM_LIMIT),
        cost_estimate=pl.CostEstimate(
            flops=16 * half * order * width, bytes_accessed=8 * order * half, transcendentals=0
        ),
    )(side, other, edge, *tables_other, left)


def pick_rows(missing, neighbours, weights, shots):
    pick = jnp.zeros((missing.shape[0], shots.shape[0]), jnp.float32)
    for slot in range(neighbours.shape[1]):
        pick = pick + jnp.where(
            neighbours[:, slot][:, None] == shots[None, :], weights[:, slot][:, None], 0.0
        )
    high = lax.reduce_precision(pick, 8, 7)
    return jnp.concatenate([high, pick - high], axis=0).astype(jnp.bfloat16)


def fill_tables(missing, neighbours, weights, start, half, edge_start, edge_rows):
    inside = start + jnp.arange(half, dtype=jnp.int32)
    beyond = edge_start + jnp.arange(edge_rows, dtype=jnp.int32)
    pick = pick_rows(missing, neighbours, weights, jnp.concatenate([inside, beyond]))
    found = inside[:, None] == missing[None, :]
    keep = 1.0 - jnp.any(found, axis=1, keepdims=True).astype(jnp.float32)
    return pick, found.astype(jnp.bfloat16), keep


def predict(records, missing, neighbours, weights, freq_bins):
    devices = lax.axis_size("shots")
    position = lax.axis_index("shots")
    shot_rows, order, samples = records.shape
    members = devices // 2
    half = order // 2
    edge_rows = shot_step(shot_rows)
    side = (position // members).astype(jnp.int32)
    groups = [list(range(members)), list(range(members, devices))]
    pairs = [(i, (i + members) % devices) for i in range(devices)]
    exchange = lambda blocks: lax.all_to_all(
        blocks, "shots", split_axis=0, concat_axis=0, axis_index_groups=groups, tiled=True
    )
    across = lambda block: lax.ppermute(block, "shots", pairs)
    widths = [order * share // sum(SHARES) for share in SHARES]
    firsts = [sum(widths[:index]) for index in range(len(widths))]
    forward, inverse = tables(freq_bins, samples)
    last_edge, next_edge = half - edge_rows, half
    own_start, other_start = side * half, (1 - side) * half
    own_edge_start = jnp.where(side == 0, last_edge, next_edge)
    other_edge_start = jnp.where(side == 0, next_edge, last_edge)
    fill = functools.partial(fill_tables, missing, neighbours, weights)
    tables_own = fill(own_start, half, other_edge_start, edge_rows)
    tables_other = fill(other_start, half, own_edge_start, edge_rows)
    own, other, edges = [], [], []
    for first, width in zip(firsts, widths):
        block = forward_chunk(records, forward, first, width)
        block = exchange(block)
        own.append(block)
        other.append(across(block))
        edges.append(
            jnp.where(side == 0, block[members - 1, :, shot_rows - edge_rows :], block[0, :, :edge_rows])
        )
    beyond = across(jnp.concatenate(edges, axis=-1))
    left = fill_own(own, beyond, tables_own, tuple(firsts))
    result = None
    for index, first in enumerate(firsts):
        predicted = product(side.reshape(1), other[index], edges[index], tables_other, left, first)
        predicted = exchange(predicted)
        result = inverse_chunk(predicted, inverse, result, first, order)
    return result


def solution(mesh):
    return jax.shard_map(
        predict,
        mesh=mesh,
        in_specs=(
            P(("lines", "shots"), None, None),
            P("lines"),
            P("lines", None),
            P("lines", None),
            P(),
        ),
        out_specs=P(("lines", "shots"), None, None),
        check_vma=False,
    )
```

```python
import functools
import math

import jax
import jax.numpy as jnp
from jax import lax
from jax.experimental import pallas as pl
from jax.experimental.pallas import tpu as pltpu
from jax.sharding import PartitionSpec as P


PARTS = 4
OUTWARD = (1, 3)
HOMEWARD = (3, 1)
STREAM_VMEM = 36 * 1024 * 1024
VMEM_LIMIT = 24 * 1024 * 1024


def tables(freq_bins, sample_count):
    bin_count = freq_bins.shape[0]
    sample_ids = jnp.arange(sample_count, dtype=jnp.int32)
    phases = freq_bins[None, :] * sample_ids[:, None] % sample_count
    angles = phases.astype(jnp.float32) * (2.0 * math.pi / sample_count)
    trig_pair = jnp.stack([jnp.cos(angles), -jnp.sin(angles)], axis=-1)
    forward = (trig_pair / math.sqrt(sample_count)).astype(jnp.bfloat16)
    inverse = (trig_pair * math.sqrt(2.0 / bin_count)).astype(jnp.bfloat16)
    rows = lambda table: jnp.transpose(table, (1, 2, 0)).reshape(2 * bin_count, sample_count)
    return rows(forward), rows(inverse)


def shot_step(shot_rows):
    return math.gcd(shot_rows, 16)


def forward_body(records_ref, table_ref, out_ref, held_ref, rows_ref, semaphores, *, first):
    pieces, step, width, samples = held_ref.shape
    planes = table_ref.shape[0]
    halves = records_ref.shape[1]
    places = [(shot * step, half) for shot in range(pieces // halves) for half in range(halves)]
    copies = [
        pltpu.make_async_copy(
            records_ref.at[pl.ds(shot, step), half, pl.ds(first, width), :],
            held_ref.at[piece],
            semaphores.at[piece],
        )
        for piece, (shot, half) in enumerate(places)
    ]
    for copy in copies:
        copy.start()
    for piece, (shot, half) in enumerate(places):
        copies[piece].wait()
        spectra = lax.dot_general(
            table_ref[...],
            held_ref[piece].reshape(step * width, samples),
            (((1,), (1,)), ((), ())),
            preferred_element_type=jnp.float32,
        )
        for row in range(step):
            rows_ref[:, row, :] = spectra[:, row * width : (row + 1) * width]
        out_ref[:, half, :, shot : shot + step, :] = (
            rows_ref[...].astype(jnp.bfloat16).reshape(planes // 2, 2, step, width)
        )


def forward_chunk(records, table, first, width):
    shot_rows, halves, _, samples = records.shape
    planes = table.shape[0]
    step = shot_step(shot_rows)
    pieces = halves * shot_rows // step
    vmem = pl.BlockSpec(memory_space=pltpu.VMEM)
    return pl.pallas_call(
        functools.partial(forward_body, first=first),
        in_specs=[pl.BlockSpec(memory_space=pl.ANY), vmem],
        out_specs=vmem,
        out_shape=jax.ShapeDtypeStruct((planes // 2, halves, 2, shot_rows, width), jnp.bfloat16),
        scratch_shapes=[
            pltpu.VMEM((pieces, step, width, samples), jnp.bfloat16),
            pltpu.VMEM((planes, step, width), jnp.float32),
            pltpu.SemaphoreType.DMA((pieces,)),
        ],
        compiler_params=pltpu.CompilerParams(vmem_limit_bytes=STREAM_VMEM),
        cost_estimate=pl.CostEstimate(
            flops=2 * shot_rows * halves * width * samples * planes,
            bytes_accessed=2 * shot_rows * halves * width * samples,
            transcendentals=0,
        ),
    )(records, table)


def inverse_body(planes_ref, table_ref, *refs, first):
    out_ref, held_ref, rows_ref, semaphores = refs[-4:]
    bins, halves, parts, _, width = planes_ref.shape
    pieces, step = held_ref.shape[:2]
    copies = []
    for piece in range(pieces):
        shot, half = piece // halves * step, piece % halves
        rows_ref[...] = (
            planes_ref[:, half, :, shot : shot + step, :]
            .astype(jnp.float32)
            .reshape(bins * parts, step, width)
        )
        for row in range(step):
            left = rows_ref[:, row, :].astype(jnp.bfloat16)
            held_ref[piece, row] = lax.dot_general(
                left, table_ref[...], (((0,), (0,)), ((), ())), preferred_element_type=jnp.float32
            ).astype(jnp.bfloat16)
        copy = pltpu.make_async_copy(
            held_ref.at[piece],
            out_ref.at[pl.ds(shot, step), half, pl.ds(first, width), :],
            semaphores.at[piece],
        )
        copy.start()
        copies.append(copy)
    for copy in copies:
        copy.wait()


def inverse_chunk(returned, table, kept, first, half):
    _, halves, _, shot_rows, width = returned.shape
    planes, samples = table.shape
    step = shot_step(shot_rows)
    pieces = halves * shot_rows // step
    vmem = pl.BlockSpec(memory_space=pltpu.VMEM)
    operands = [returned, table] + ([] if kept is None else [kept])
    return pl.pallas_call(
        functools.partial(inverse_body, first=first),
        in_specs=[vmem, vmem] + [pl.BlockSpec(memory_space=pl.ANY)] * (len(operands) - 2),
        out_specs=pl.BlockSpec(memory_space=pl.ANY),
        out_shape=jax.ShapeDtypeStruct((shot_rows, halves, half, samples), jnp.bfloat16),
        scratch_shapes=[
            pltpu.VMEM((pieces, step, width, samples), jnp.bfloat16),
            pltpu.VMEM((planes, step, width), jnp.float32),
            pltpu.SemaphoreType.DMA((pieces,)),
        ],
        input_output_aliases={} if kept is None else {2: 0},
        compiler_params=pltpu.CompilerParams(vmem_limit_bytes=STREAM_VMEM),
        cost_estimate=pl.CostEstimate(
            flops=2 * shot_rows * halves * width * samples * planes,
            bytes_accessed=2 * shot_rows * halves * width * samples,
            transcendentals=0,
        ),
    )(*operands)


def fill_body(spectra_ref, pick_ref, place_ref, keep_ref, out_ref):
    devices, parts, rows, width = spectra_ref.shape
    count = pick_ref.shape[0] // 2
    for part in range(parts):
        recorded = spectra_ref[:, part].reshape(devices * rows, width)
        both = jnp.dot(pick_ref[...], recorded, preferred_element_type=jnp.float32)
        replaced = (both[:count] + both[count:]).astype(jnp.bfloat16)
        placed = jnp.dot(place_ref[...], replaced, preferred_element_type=jnp.float32)
        out_ref[part] = (placed + recorded.astype(jnp.float32) * keep_ref[...]).astype(jnp.bfloat16)


def fill(spectra, pick, place, keep):
    devices, parts, rows, width = spectra.shape
    order = devices * rows
    return pl.pallas_call(
        fill_body,
        out_shape=jax.ShapeDtypeStruct((parts, order, width), jnp.bfloat16),
        compiler_params=pltpu.CompilerParams(vmem_limit_bytes=VMEM_LIMIT),
        cost_estimate=pl.CostEstimate(
            flops=8 * pick.shape[0] * order * width,
            bytes_accessed=8 * order * width,
            transcendentals=0,
        ),
        name="fill",
    )(spectra, pick, place, keep)


def product_body(member_ref, *refs, count, first, scale):
    sources, out_ref, right_ref = refs[: 2 * count], refs[2 * count], refs[2 * count + 1]
    devices, parts, rows, width = out_ref.shape
    order = devices * rows
    half = order // 2
    member = member_ref[0]
    spans = []
    start = 0
    for ref in sources[:count]:
        size = ref.shape[2]
        low, high = max(start, first), min(start + size, first + width)
        if low < high:
            spans.append((ref, low - start, low - first, high - low))
        start += size
    for ref, begin, at, size in spans:
        real = ref[0, :, begin : begin + size]
        imag = ref[1, :, begin : begin + size]
        right_ref[0, :, at : at + size] = real
        right_ref[0, :, width + at : width + at + size] = imag
        right_ref[1, :, at : at + size] = -imag
        right_ref[1, :, width + at : width + at + size] = real
    total = None
    for owner in range(2):
        offset = (member if owner == 0 else 1 - member) * half
        for part in range(parts):
            start = 0
            for ref in sources[owner * count : (owner + 1) * count]:
                size = ref.shape[2]
                rows_at = pl.multiple_of(offset + start, 128)
                term = jnp.dot(
                    ref[part], right_ref[part, pl.ds(rows_at, size), :], preferred_element_type=jnp.float32
                )
                total = term if total is None else total + term
                start += size
    total = total * scale
    for part in range(parts):
        out_ref[:, part] = (
            total[:, part * width : (part + 1) * width]
            .astype(jnp.bfloat16)
            .reshape(devices, rows, width)
        )


def product(member, own, other, first, width, devices):
    parts, order, _ = own[0].shape
    vmem = pl.BlockSpec(memory_space=pltpu.VMEM)
    return pl.pallas_call(
        functools.partial(
            product_body, count=len(own), first=first, scale=-1.0 / math.sqrt(order)
        ),
        in_specs=[pl.BlockSpec(memory_space=pltpu.SMEM)] + [vmem] * (2 * len(own)),
        out_specs=vmem,
        out_shape=jax.ShapeDtypeStruct((devices, parts, order // devices, width), jnp.bfloat16),
        scratch_shapes=[pltpu.VMEM((parts, order, 2 * width), jnp.bfloat16)],
        compiler_params=pltpu.CompilerParams(vmem_limit_bytes=VMEM_LIMIT),
        cost_estimate=pl.CostEstimate(
            flops=16 * order * order * width, bytes_accessed=8 * order * order, transcendentals=0
        ),
    )(member, *own, *other)


def fill_tables(missing, neighbours, weights, order):
    shots = jnp.arange(order, dtype=jnp.int32)
    pick = jnp.zeros((missing.shape[0], order), jnp.float32)
    for slot in range(neighbours.shape[1]):
        pick = pick + jnp.where(
            neighbours[:, slot][:, None] == shots[None, :], weights[:, slot][:, None], 0.0
        )
    high = lax.reduce_precision(pick, 8, 7)
    found = shots[:, None] == missing[None, :]
    keep = 1.0 - jnp.any(found, axis=1, keepdims=True).astype(jnp.float32)
    both = jnp.concatenate([high, pick - high], axis=0).astype(jnp.bfloat16)
    return both, found.astype(jnp.bfloat16), keep


def spread(total, shares):
    widths = [total * share // PARTS for share in shares]
    return [(sum(widths[:index]), width) for index, width in enumerate(widths)]


def predict(records, missing, neighbours, weights, freq_bins):
    devices = lax.axis_size("shots")
    position = lax.axis_index("shots")
    shot_rows, order, samples = records.shape
    half = order // 2
    bins = freq_bins.shape[0]
    member = (position % 2).astype(jnp.int32).reshape(1)
    pairs = [(i, i ^ 1) for i in range(devices)]

    def exchange(blocks):
        return lax.all_to_all(blocks, "shots", split_axis=0, concat_axis=0, tiled=True)

    forward, inverse = tables(freq_bins, samples)
    pick, place, keep = fill_tables(missing, neighbours, weights, order)
    split = records.reshape(shot_rows, 2, half, samples)
    own, other = [], []
    for first, width in spread(half, OUTWARD):
        block = forward_chunk(split, forward, first, width)
        block = exchange(block.reshape(devices, 2, shot_rows, width))
        block = fill(block, pick, place, keep)
        own.append(block)
        other.append(lax.ppermute(block, "shots", pairs))
    result = None
    for first, width in spread(half, HOMEWARD):
        block = product(member, own, other, first, width, devices)
        block = exchange(block)
        block = block.reshape(bins, 2, 2, shot_rows, width)
        result = inverse_chunk(block, inverse, result, first, half)
    return result.reshape(shot_rows, order, samples)


def solution(mesh):
    return jax.shard_map(
        predict,
        mesh=mesh,
        in_specs=(
            P(("lines", "shots"), None, None),
            P("lines"),
            P("lines", None),
            P("lines", None),
            P(),
        ),
        out_specs=P(("lines", "shots"), None, None),
        check_vma=False,
    )
```

```python
import functools
import math

import jax
import jax.numpy as jnp
from jax import lax
from jax.experimental import pallas as pl
from jax.experimental.pallas import tpu as pltpu
from jax.sharding import PartitionSpec as P


PARTS = 4
OUTWARD = (1, 3)
HOMEWARD = (1, 2, 1)
LOOSE = 1
LOOSE_DEVICES = 16
STREAM_VMEM = 36 * 1024 * 1024
VMEM_LIMIT = 24 * 1024 * 1024


def tables(freq_bins, sample_count):
    bin_count = freq_bins.shape[0]
    sample_ids = jnp.arange(sample_count, dtype=jnp.int32)
    phases = freq_bins[None, :] * sample_ids[:, None] % sample_count
    angles = phases.astype(jnp.float32) * (2.0 * math.pi / sample_count)
    trig_pair = jnp.stack([jnp.cos(angles), -jnp.sin(angles)], axis=-1)
    forward = (trig_pair / math.sqrt(sample_count)).astype(jnp.bfloat16)
    inverse = (trig_pair * math.sqrt(2.0 / bin_count)).astype(jnp.bfloat16)
    rows = lambda table: jnp.transpose(table, (1, 2, 0)).reshape(2 * bin_count, sample_count)
    return rows(forward), rows(inverse)


def shot_step(shot_rows):
    return math.gcd(shot_rows, 16)


def forward_body(records_ref, table_ref, out_ref, held_ref, rows_ref, semaphores, *, first):
    pieces, step, width, samples = held_ref.shape
    planes = table_ref.shape[0]
    halves = records_ref.shape[1]
    places = [(shot * step, half) for shot in range(pieces // halves) for half in range(halves)]
    copies = [
        pltpu.make_async_copy(
            records_ref.at[pl.ds(shot, step), half, pl.ds(first, width), :],
            held_ref.at[piece],
            semaphores.at[piece],
        )
        for piece, (shot, half) in enumerate(places)
    ]
    for copy in copies:
        copy.start()
    for piece, (shot, half) in enumerate(places):
        copies[piece].wait()
        spectra = lax.dot_general(
            table_ref[...],
            held_ref[piece].reshape(step * width, samples),
            (((1,), (1,)), ((), ())),
            preferred_element_type=jnp.float32,
        )
        for row in range(step):
            rows_ref[:, row, :] = spectra[:, row * width : (row + 1) * width]
        out_ref[:, half, :, shot : shot + step, :] = (
            rows_ref[...].astype(jnp.bfloat16).reshape(planes // 2, 2, step, width)
        )


def forward_chunk(records, table, first, width):
    shot_rows, halves, _, samples = records.shape
    planes = table.shape[0]
    step = shot_step(shot_rows)
    pieces = halves * shot_rows // step
    vmem = pl.BlockSpec(memory_space=pltpu.VMEM)
    return pl.pallas_call(
        functools.partial(forward_body, first=first),
        in_specs=[pl.BlockSpec(memory_space=pl.ANY), vmem],
        out_specs=vmem,
        out_shape=jax.ShapeDtypeStruct((planes // 2, halves, 2, shot_rows, width), jnp.bfloat16),
        scratch_shapes=[
            pltpu.VMEM((pieces, step, width, samples), jnp.bfloat16),
            pltpu.VMEM((planes, step, width), jnp.float32),
            pltpu.SemaphoreType.DMA((pieces,)),
        ],
        compiler_params=pltpu.CompilerParams(vmem_limit_bytes=STREAM_VMEM),
        cost_estimate=pl.CostEstimate(
            flops=2 * shot_rows * halves * width * samples * planes,
            bytes_accessed=2 * shot_rows * halves * width * samples,
            transcendentals=0,
        ),
    )(records, table)


def inverse_body(planes_ref, table_ref, *refs, first):
    out_ref, held_ref, rows_ref, semaphores = refs[-4:]
    bins, halves, parts, _, width = planes_ref.shape
    pieces, step = held_ref.shape[:2]
    copies = []
    for piece in range(pieces):
        shot, half = piece // halves * step, piece % halves
        rows_ref[...] = (
            planes_ref[:, half, :, shot : shot + step, :]
            .astype(jnp.float32)
            .reshape(bins * parts, step, width)
        )
        for row in range(step):
            left = rows_ref[:, row, :].astype(jnp.bfloat16)
            held_ref[piece, row] = lax.dot_general(
                left, table_ref[...], (((0,), (0,)), ((), ())), preferred_element_type=jnp.float32
            ).astype(jnp.bfloat16)
        copy = pltpu.make_async_copy(
            held_ref.at[piece],
            out_ref.at[pl.ds(shot, step), half, pl.ds(first, width), :],
            semaphores.at[piece],
        )
        copy.start()
        copies.append(copy)
    for copy in copies:
        copy.wait()


def inverse_chunk(returned, table, kept, first, half):
    _, halves, _, shot_rows, width = returned.shape
    planes, samples = table.shape
    step = shot_step(shot_rows)
    pieces = halves * shot_rows // step
    vmem = pl.BlockSpec(memory_space=pltpu.VMEM)
    operands = [returned, table] + ([] if kept is None else [kept])
    return pl.pallas_call(
        functools.partial(inverse_body, first=first),
        in_specs=[vmem, vmem] + [pl.BlockSpec(memory_space=pl.ANY)] * (len(operands) - 2),
        out_specs=pl.BlockSpec(memory_space=pl.ANY),
        out_shape=jax.ShapeDtypeStruct((shot_rows, halves, half, samples), jnp.bfloat16),
        scratch_shapes=[
            pltpu.VMEM((pieces, step, width, samples), jnp.bfloat16),
            pltpu.VMEM((planes, step, width), jnp.float32),
            pltpu.SemaphoreType.DMA((pieces,)),
        ],
        input_output_aliases={} if kept is None else {2: 0},
        compiler_params=pltpu.CompilerParams(vmem_limit_bytes=STREAM_VMEM),
        cost_estimate=pl.CostEstimate(
            flops=2 * shot_rows * halves * width * samples * planes,
            bytes_accessed=2 * shot_rows * halves * width * samples,
            transcendentals=0,
        ),
    )(*operands)


def loose_body(place_ref, table_ref, kept_ref, *refs, first):
    pieces_refs, (out_ref, held_ref, planes_ref, semaphores) = refs[:-4], refs[-4:]
    pieces, step = held_ref.shape[:2]
    halves = out_ref.shape[1]
    position = place_ref[0]
    for index, piece_ref in enumerate(pieces_refs):
        source = jnp.bitwise_xor(position, index)
        for part in range(piece_ref.shape[0]):
            planes_ref[source % 2, source // 2 * 2 + part] = piece_ref[part].astype(jnp.float32)
    copies = []
    for piece in range(pieces):
        shot, half = piece // halves * step, piece % halves
        for row in range(step):
            left = planes_ref[half, :, shot + row, :].astype(jnp.bfloat16)
            held_ref[piece, row] = lax.dot_general(
                left, table_ref[...], (((0,), (0,)), ((), ())), preferred_element_type=jnp.float32
            ).astype(jnp.bfloat16)
        copy = pltpu.make_async_copy(
            held_ref.at[piece],
            out_ref.at[pl.ds(shot, step), half, pl.ds(first, held_ref.shape[2]), :],
            semaphores.at[piece],
        )
        copy.start()
        copies.append(copy)
    for copy in copies:
        copy.wait()


def loose_inverse(place, returned, table, kept, first):
    _, shot_rows, width = returned[0].shape
    halves = kept.shape[1]
    planes, samples = table.shape
    step = shot_step(shot_rows)
    pieces = halves * shot_rows // step
    vmem = pl.BlockSpec(memory_space=pltpu.VMEM)
    anywhere = pl.BlockSpec(memory_space=pl.ANY)
    return pl.pallas_call(
        functools.partial(loose_body, first=first),
        in_specs=[pl.BlockSpec(memory_space=pltpu.SMEM), vmem, anywhere] + [vmem] * len(returned),
        out_specs=anywhere,
        out_shape=jax.ShapeDtypeStruct(kept.shape, kept.dtype),
        scratch_shapes=[
            pltpu.VMEM((pieces, step, width, samples), jnp.bfloat16),
            pltpu.VMEM((halves, planes, shot_rows, width), jnp.float32),
            pltpu.SemaphoreType.DMA((pieces,)),
        ],
        input_output_aliases={2: 0},
        compiler_params=pltpu.CompilerParams(vmem_limit_bytes=STREAM_VMEM),
        cost_estimate=pl.CostEstimate(
            flops=2 * shot_rows * halves * width * samples * planes,
            bytes_accessed=2 * shot_rows * halves * width * samples,
            transcendentals=0,
        ),
    )(place, table, kept, *returned)


def fill_body(spectra_ref, pick_ref, place_ref, keep_ref, out_ref):
    devices, parts, rows, width = spectra_ref.shape
    count = pick_ref.shape[0] // 2
    for part in range(parts):
        recorded = spectra_ref[:, part].reshape(devices * rows, width)
        both = jnp.dot(pick_ref[...], recorded, preferred_element_type=jnp.float32)
        replaced = (both[:count] + both[count:]).astype(jnp.bfloat16)
        placed = jnp.dot(place_ref[...], replaced, preferred_element_type=jnp.float32)
        out_ref[:, part * width : (part + 1) * width] = (
            placed + recorded.astype(jnp.float32) * keep_ref[...]
        ).astype(jnp.bfloat16)


def fill(spectra, pick, place, keep):
    devices, parts, rows, width = spectra.shape
    order = devices * rows
    return pl.pallas_call(
        fill_body,
        out_shape=jax.ShapeDtypeStruct((order, parts * width), jnp.bfloat16),
        compiler_params=pltpu.CompilerParams(vmem_limit_bytes=VMEM_LIMIT),
        cost_estimate=pl.CostEstimate(
            flops=8 * pick.shape[0] * order * width,
            bytes_accessed=8 * order * width,
            transcendentals=0,
        ),
        name="fill",
    )(spectra, pick, place, keep)


def product_body(place_ref, *refs, count, first, width, scale, loose):
    sources, out_refs, right_ref, total_ref = refs[: 2 * count], refs[2 * count : -2], refs[-2], refs[-1]
    order = right_ref.shape[0] // 2
    half = order // 2
    position = place_ref[0]
    member = position % 2
    spans = []
    start = 0
    for ref in sources[:count]:
        size = ref.shape[1] // 2
        low, high = max(start, first), min(start + size, first + width)
        if low < high:
            spans.append((ref, size, low - start, low - first, high - low))
        start += size
    line = 0
    for owner in range(2):
        offset = (member if owner == 0 else 1 - member) * half
        start = 0
        for source in sources[:count]:
            rows = source.shape[1] // 2
            lines = pl.ds(pl.multiple_of(offset + start, 128), rows)
            for ref, size, begin, at, span in spans:
                real = ref[lines, begin : begin + span]
                imag = ref[lines, size + begin : size + begin + span]
                right_ref[line : line + rows, at : at + span] = real
                right_ref[line : line + rows, width + at : width + at + span] = imag
                right_ref[line + rows : line + 2 * rows, at : at + span] = -imag
                right_ref[line + rows : line + 2 * rows, width + at : width + at + span] = real
            line += 2 * rows
            start += rows
    block = math.gcd(order, 256)
    for row in range(0, order, block):
        total = None
        line = 0
        for ref in sources:
            depth = ref.shape[1]
            term = jnp.dot(
                ref[row : row + block], right_ref[line : line + depth], preferred_element_type=jnp.float32
            )
            total = term if total is None else total + term
            line += depth
        total_ref[row : row + block] = (total * scale).astype(jnp.bfloat16)
    if loose:
        rows = order // len(out_refs)
        for index, out_ref in enumerate(out_refs):
            target = jnp.bitwise_xor(position, index)
            lines = pl.ds(pl.multiple_of(target * rows, rows), rows)
            for part in range(2):
                out_ref[part] = total_ref[lines, part * width : (part + 1) * width]
    else:
        (out_ref,) = out_refs
        devices, parts, rows, _ = out_ref.shape
        for part in range(parts):
            out_ref[:, part] = total_ref[:, part * width : (part + 1) * width].reshape(
                devices, rows, width
            )


def product(place, own, other, first, width, devices, loose):
    order, _ = own[0].shape
    rows = order // devices
    vmem = pl.BlockSpec(memory_space=pltpu.VMEM)
    shape = jax.ShapeDtypeStruct((devices, 2, rows, width), jnp.bfloat16)
    if loose:
        shape = [jax.ShapeDtypeStruct((2, rows, width), jnp.bfloat16)] * devices
    return pl.pallas_call(
        functools.partial(
            product_body,
            count=len(own),
            first=first,
            width=width,
            scale=-1.0 / math.sqrt(order),
            loose=loose,
        ),
        in_specs=[pl.BlockSpec(memory_space=pltpu.SMEM)] + [vmem] * (2 * len(own)),
        out_specs=[vmem] * devices if loose else vmem,
        out_shape=shape,
        scratch_shapes=[
            pltpu.VMEM((2 * order, 2 * width), jnp.bfloat16),
            pltpu.VMEM((order, 2 * width), jnp.bfloat16),
        ],
        compiler_params=pltpu.CompilerParams(vmem_limit_bytes=VMEM_LIMIT),
        cost_estimate=pl.CostEstimate(
            flops=16 * order * order * width, bytes_accessed=8 * order * order, transcendentals=0
        ),
    )(place, *own, *other)


def fill_tables(missing, neighbours, weights, order):
    shots = jnp.arange(order, dtype=jnp.int32)
    pick = jnp.zeros((missing.shape[0], order), jnp.float32)
    for slot in range(neighbours.shape[1]):
        pick = pick + jnp.where(
            neighbours[:, slot][:, None] == shots[None, :], weights[:, slot][:, None], 0.0
        )
    high = lax.reduce_precision(pick, 8, 7)
    found = shots[:, None] == missing[None, :]
    keep = 1.0 - jnp.any(found, axis=1, keepdims=True).astype(jnp.float32)
    both = jnp.concatenate([high, pick - high], axis=0).astype(jnp.bfloat16)
    return both, found.astype(jnp.bfloat16), keep


def spread(total, shares):
    widths = [total * share // PARTS for share in shares]
    return [(sum(widths[:index]), width) for index, width in enumerate(widths)]


def predict(records, missing, neighbours, weights, freq_bins):
    devices = lax.axis_size("shots")
    position = lax.axis_index("shots")
    shot_rows, order, samples = records.shape
    half = order // 2
    bins = freq_bins.shape[0]
    place_of = position.astype(jnp.int32).reshape(1)
    pairs = [(i, i ^ 1) for i in range(devices)]

    def exchange(blocks):
        return lax.all_to_all(blocks, "shots", split_axis=0, concat_axis=0, tiled=True)

    forward, inverse = tables(freq_bins, samples)
    pick, place, keep = fill_tables(missing, neighbours, weights, order)
    split = records.reshape(shot_rows, 2, half, samples)
    own, other = [], []
    for first, width in spread(half, OUTWARD):
        block = forward_chunk(split, forward, first, width)
        block = exchange(block.reshape(devices, 2, shot_rows, width))
        block = fill(block, pick, place, keep)
        own.append(block)
        other.append(lax.ppermute(block, "shots", pairs))
    result = None
    for index, (first, width) in enumerate(spread(half, HOMEWARD)):
        loose = index == LOOSE and devices <= LOOSE_DEVICES
        block = product(place_of, own, other, first, width, devices, loose)
        if loose:
            arrived = [block[0]]
            for step in range(1, devices):
                route = [(i, i ^ step) for i in range(devices)]
                arrived.append(lax.ppermute(block[step], "shots", route))
            result = loose_inverse(place_of, arrived, inverse, result, first)
        else:
            block = exchange(block)
            block = block.reshape(bins, 2, 2, shot_rows, width)
            result = inverse_chunk(block, inverse, result, first, half)
    return result.reshape(shot_rows, order, samples)


def solution(mesh):
    return jax.shard_map(
        predict,
        mesh=mesh,
        in_specs=(
            P(("lines", "shots"), None, None),
            P("lines"),
            P("lines", None),
            P("lines", None),
            P(),
        ),
        out_specs=P(("lines", "shots"), None, None),
        check_vma=False,
    )
```

```python
import functools
import math

import jax
import jax.numpy as jnp
from jax import lax
from jax.experimental import pallas as pl
from jax.experimental.pallas import tpu as pltpu
from jax.sharding import PartitionSpec as P


PARTS = 4
OUTWARD = (1, 3)
HOMEWARD = (1, 2, 1)
LOOSE = 1
LOOSE_DEVICES = 16
STREAM_VMEM = 36 * 1024 * 1024
VMEM_LIMIT = 24 * 1024 * 1024


def tables(freq_bins, sample_count):
    bin_count = freq_bins.shape[0]
    sample_ids = jnp.arange(sample_count, dtype=jnp.int32)
    phases = freq_bins[None, :] * sample_ids[:, None] % sample_count
    angles = phases.astype(jnp.float32) * (2.0 * math.pi / sample_count)
    trig_pair = jnp.stack([jnp.cos(angles), -jnp.sin(angles)], axis=-1)
    forward = (trig_pair / math.sqrt(sample_count)).astype(jnp.bfloat16)
    inverse = (trig_pair * math.sqrt(2.0 / bin_count)).astype(jnp.bfloat16)
    rows = lambda table: jnp.transpose(table, (1, 2, 0)).reshape(2 * bin_count, sample_count)
    return rows(forward), rows(inverse)


def shot_step(shot_rows):
    return math.gcd(shot_rows, 16)


def forward_body(records_ref, table_ref, out_ref, held_ref, rows_ref, semaphores, *, first):
    pieces, step, width, samples = held_ref.shape
    planes = table_ref.shape[0]
    halves = records_ref.shape[1]
    places = [(shot * step, half) for shot in range(pieces // halves) for half in range(halves)]
    copies = [
        pltpu.make_async_copy(
            records_ref.at[pl.ds(shot, step), half, pl.ds(first, width), :],
            held_ref.at[piece],
            semaphores.at[piece],
        )
        for piece, (shot, half) in enumerate(places)
    ]
    for copy in copies:
        copy.start()
    for piece, (shot, half) in enumerate(places):
        copies[piece].wait()
        spectra = lax.dot_general(
            table_ref[...],
            held_ref[piece].reshape(step * width, samples),
            (((1,), (1,)), ((), ())),
            preferred_element_type=jnp.float32,
        )
        for row in range(step):
            rows_ref[:, row, :] = spectra[:, row * width : (row + 1) * width]
        out_ref[:, half, :, shot : shot + step, :] = (
            rows_ref[...].astype(jnp.bfloat16).reshape(planes // 2, 2, step, width)
        )


def forward_chunk(records, table, first, width):
    shot_rows, halves, _, samples = records.shape
    planes = table.shape[0]
    step = shot_step(shot_rows)
    pieces = halves * shot_rows // step
    vmem = pl.BlockSpec(memory_space=pltpu.VMEM)
    return pl.pallas_call(
        functools.partial(forward_body, first=first),
        in_specs=[pl.BlockSpec(memory_space=pl.ANY), vmem],
        out_specs=vmem,
        out_shape=jax.ShapeDtypeStruct((planes // 2, halves, 2, shot_rows, width), jnp.bfloat16),
        scratch_shapes=[
            pltpu.VMEM((pieces, step, width, samples), jnp.bfloat16),
            pltpu.VMEM((planes, step, width), jnp.float32),
            pltpu.SemaphoreType.DMA((pieces,)),
        ],
        compiler_params=pltpu.CompilerParams(vmem_limit_bytes=STREAM_VMEM),
        cost_estimate=pl.CostEstimate(
            flops=2 * shot_rows * halves * width * samples * planes,
            bytes_accessed=2 * shot_rows * halves * width * samples,
            transcendentals=0,
        ),
    )(records, table)


def inverse_body(planes_ref, table_ref, *refs, first):
    out_ref, held_ref, rows_ref, semaphores = refs[-4:]
    bins, halves, parts, _, width = planes_ref.shape
    pieces, step = held_ref.shape[:2]
    copies = []
    for piece in range(pieces):
        shot, half = piece // halves * step, piece % halves
        rows_ref[...] = (
            planes_ref[:, half, :, shot : shot + step, :]
            .astype(jnp.float32)
            .reshape(bins * parts, step, width)
        )
        for row in range(step):
            left = rows_ref[:, row, :].astype(jnp.bfloat16)
            held_ref[piece, row] = lax.dot_general(
                left, table_ref[...], (((0,), (0,)), ((), ())), preferred_element_type=jnp.float32
            ).astype(jnp.bfloat16)
        copy = pltpu.make_async_copy(
            held_ref.at[piece],
            out_ref.at[pl.ds(shot, step), half, pl.ds(first, width), :],
            semaphores.at[piece],
        )
        copy.start()
        copies.append(copy)
    for copy in copies:
        copy.wait()


def inverse_chunk(returned, table, kept, first, half):
    _, halves, _, shot_rows, width = returned.shape
    planes, samples = table.shape
    step = shot_step(shot_rows)
    pieces = halves * shot_rows // step
    vmem = pl.BlockSpec(memory_space=pltpu.VMEM)
    operands = [returned, table] + ([] if kept is None else [kept])
    return pl.pallas_call(
        functools.partial(inverse_body, first=first),
        in_specs=[vmem, vmem] + [pl.BlockSpec(memory_space=pl.ANY)] * (len(operands) - 2),
        out_specs=pl.BlockSpec(memory_space=pl.ANY),
        out_shape=jax.ShapeDtypeStruct((shot_rows, halves, half, samples), jnp.bfloat16),
        scratch_shapes=[
            pltpu.VMEM((pieces, step, width, samples), jnp.bfloat16),
            pltpu.VMEM((planes, step, width), jnp.float32),
            pltpu.SemaphoreType.DMA((pieces,)),
        ],
        input_output_aliases={} if kept is None else {2: 0},
        compiler_params=pltpu.CompilerParams(vmem_limit_bytes=STREAM_VMEM),
        cost_estimate=pl.CostEstimate(
            flops=2 * shot_rows * halves * width * samples * planes,
            bytes_accessed=2 * shot_rows * halves * width * samples,
            transcendentals=0,
        ),
    )(*operands)


def loose_body(place_ref, table_ref, kept_ref, *refs, first):
    pieces_refs, (out_ref, held_ref, planes_ref, semaphores) = refs[:-4], refs[-4:]
    pieces, step = held_ref.shape[:2]
    halves = out_ref.shape[1]
    position = place_ref[0]
    for index, piece_ref in enumerate(pieces_refs):
        source = jnp.bitwise_xor(position, index)
        for part in range(piece_ref.shape[0]):
            planes_ref[source % 2, source // 2 * 2 + part] = piece_ref[part].astype(jnp.float32)
    copies = []
    for piece in range(pieces):
        shot, half = piece // halves * step, piece % halves
        for row in range(step):
            left = planes_ref[half, :, shot + row, :].astype(jnp.bfloat16)
            held_ref[piece, row] = lax.dot_general(
                left, table_ref[...], (((0,), (0,)), ((), ())), preferred_element_type=jnp.float32
            ).astype(jnp.bfloat16)
        copy = pltpu.make_async_copy(
            held_ref.at[piece],
            out_ref.at[pl.ds(shot, step), half, pl.ds(first, held_ref.shape[2]), :],
            semaphores.at[piece],
        )
        copy.start()
        copies.append(copy)
    for copy in copies:
        copy.wait()


def loose_inverse(place, returned, table, kept, first):
    _, shot_rows, width = returned[0].shape
    halves = kept.shape[1]
    planes, samples = table.shape
    step = shot_step(shot_rows)
    pieces = halves * shot_rows // step
    vmem = pl.BlockSpec(memory_space=pltpu.VMEM)
    anywhere = pl.BlockSpec(memory_space=pl.ANY)
    return pl.pallas_call(
        functools.partial(loose_body, first=first),
        in_specs=[pl.BlockSpec(memory_space=pltpu.SMEM), vmem, anywhere] + [vmem] * len(returned),
        out_specs=anywhere,
        out_shape=jax.ShapeDtypeStruct(kept.shape, kept.dtype),
        scratch_shapes=[
            pltpu.VMEM((pieces, step, width, samples), jnp.bfloat16),
            pltpu.VMEM((halves, planes, shot_rows, width), jnp.float32),
            pltpu.SemaphoreType.DMA((pieces,)),
        ],
        input_output_aliases={2: 0},
        compiler_params=pltpu.CompilerParams(vmem_limit_bytes=STREAM_VMEM),
        cost_estimate=pl.CostEstimate(
            flops=2 * shot_rows * halves * width * samples * planes,
            bytes_accessed=2 * shot_rows * halves * width * samples,
            transcendentals=0,
        ),
    )(place, table, kept, *returned)


def fill_into(out_ref, spectra_ref, pick_ref, put_ref, keep_ref):
    devices, parts, rows, width = spectra_ref.shape
    count = pick_ref.shape[0] // 2
    for part in range(parts):
        recorded = spectra_ref[:, part].reshape(devices * rows, width)
        both = jnp.dot(pick_ref[...], recorded, preferred_element_type=jnp.float32)
        replaced = (both[:count] + both[count:]).astype(jnp.bfloat16)
        placed = jnp.dot(put_ref[...], replaced, preferred_element_type=jnp.float32)
        out_ref[:, part * width : (part + 1) * width] = placed.astype(jnp.bfloat16) + recorded * keep_ref[
            ...
        ].astype(jnp.bfloat16)


def fill_body(spectra_ref, pick_ref, put_ref, keep_ref, out_ref):
    fill_into(out_ref, spectra_ref, pick_ref, put_ref, keep_ref)


def fill(spectra, pick, place, keep):
    devices, parts, rows, width = spectra.shape
    order = devices * rows
    return pl.pallas_call(
        fill_body,
        out_shape=jax.ShapeDtypeStruct((order, parts * width), jnp.bfloat16),
        compiler_params=pltpu.CompilerParams(vmem_limit_bytes=VMEM_LIMIT),
        cost_estimate=pl.CostEstimate(
            flops=8 * pick.shape[0] * order * width,
            bytes_accessed=8 * order * width,
            transcendentals=0,
        ),
        name="fill",
    )(spectra, pick, place, keep)


def product_body(place_ref, *refs, count, first, width, scale, loose):
    sources, out_refs, right_ref, total_ref = refs[: 2 * count], refs[2 * count : -2], refs[-2], refs[-1]
    order = right_ref.shape[0] // 2
    half = order // 2
    position = place_ref[0]
    member = position % 2
    spans = []
    start = 0
    for ref in sources[:count]:
        size = ref.shape[1] // 2
        low, high = max(start, first), min(start + size, first + width)
        if low < high:
            spans.append((ref, size, low - start, low - first, high - low))
        start += size
    line = 0
    for owner in range(2):
        offset = (member if owner == 0 else 1 - member) * half
        start = 0
        for source in sources[:count]:
            rows = source.shape[1] // 2
            lines = pl.ds(pl.multiple_of(offset + start, 128), rows)
            for ref, size, begin, at, span in spans:
                real = ref[lines, begin : begin + span]
                imag = ref[lines, size + begin : size + begin + span]
                right_ref[line : line + rows, at : at + span] = real
                right_ref[line : line + rows, width + at : width + at + span] = imag
                right_ref[line + rows : line + 2 * rows, at : at + span] = -imag
                right_ref[line + rows : line + 2 * rows, width + at : width + at + span] = real
            line += 2 * rows
            start += rows
    block = math.gcd(order, 256)
    for row in range(0, order, block):
        total = None
        line = 0
        for ref in sources:
            depth = ref.shape[1]
            term = jnp.dot(
                ref[row : row + block], right_ref[line : line + depth], preferred_element_type=jnp.float32
            )
            total = term if total is None else total + term
            line += depth
        total_ref[row : row + block] = (total * scale).astype(jnp.bfloat16)
    if loose:
        rows = order // len(out_refs)
        for index, out_ref in enumerate(out_refs):
            target = jnp.bitwise_xor(position, index)
            lines = pl.ds(pl.multiple_of(target * rows, rows), rows)
            for part in range(2):
                out_ref[part] = total_ref[lines, part * width : (part + 1) * width]
    else:
        (out_ref,) = out_refs
        devices, parts, rows, _ = out_ref.shape
        for part in range(parts):
            out_ref[:, part] = total_ref[:, part * width : (part + 1) * width].reshape(
                devices, rows, width
            )


def product(place, own, other, first, width, devices, loose):
    order, _ = own[0].shape
    rows = order // devices
    vmem = pl.BlockSpec(memory_space=pltpu.VMEM)
    shape = jax.ShapeDtypeStruct((devices, 2, rows, width), jnp.bfloat16)
    if loose:
        shape = [jax.ShapeDtypeStruct((2, rows, width), jnp.bfloat16)] * devices
    return pl.pallas_call(
        functools.partial(
            product_body,
            count=len(own),
            first=first,
            width=width,
            scale=-1.0 / math.sqrt(order),
            loose=loose,
        ),
        in_specs=[pl.BlockSpec(memory_space=pltpu.SMEM)] + [vmem] * (2 * len(own)),
        out_specs=[vmem] * devices if loose else vmem,
        out_shape=shape,
        scratch_shapes=[
            pltpu.VMEM((2 * order, 2 * width), jnp.bfloat16),
            pltpu.VMEM((order, 2 * width), jnp.bfloat16),
        ],
        compiler_params=pltpu.CompilerParams(vmem_limit_bytes=VMEM_LIMIT),
        cost_estimate=pl.CostEstimate(
            flops=16 * order * order * width, bytes_accessed=8 * order * order, transcendentals=0
        ),
    )(place, *own, *other)


def opening_body(place_ref, spectra_ref, pick_ref, put_ref, keep_ref, *refs, sources, scale):
    source_refs, refs = refs[:sources], refs[sources:]
    out_ref, filled_ref = refs[:2]
    held_refs, (right_ref, semaphores) = refs[2:-2], refs[-2:]
    copies = [
        pltpu.make_async_copy(source, held, semaphores.at[index])
        for index, (source, held) in enumerate(zip(source_refs, held_refs))
    ]
    for copy in copies:
        copy.start()
    fill_into(filled_ref, spectra_ref, pick_ref, put_ref, keep_ref)
    for copy in copies:
        copy.wait()
    order = filled_ref.shape[0]
    half = order // 2
    _, parts, rows, width = out_ref.shape
    count = (sources + 1) // 2
    lefts = list(held_refs) + [filled_ref]
    own_ref = held_refs[0]
    member = place_ref[0] % 2
    line = 0
    for index, left in enumerate(lefts):
        if index % count == 0:
            start = (member if index == 0 else 1 - member) * half
        depth = left.shape[1] // 2
        lines = pl.ds(pl.multiple_of(start, 128), depth)
        real = own_ref[lines, :width]
        imag = own_ref[lines, width:]
        right_ref[line : line + depth, :width] = real
        right_ref[line : line + depth, width:] = imag
        right_ref[line + depth : line + 2 * depth, :width] = -imag
        right_ref[line + depth : line + 2 * depth, width:] = real
        line += 2 * depth
        start += depth
    block = math.gcd(order, 256)
    for row in range(0, order, block):
        total = None
        line = 0
        for left in lefts:
            depth = left.shape[1]
            term = jnp.dot(
                left[row : row + block], right_ref[line : line + depth], preferred_element_type=jnp.float32
            )
            total = term if total is None else total + term
            line += depth
        total = (total * scale).astype(jnp.bfloat16)
        first = row // rows
        for part in range(parts):
            out_ref[first : first + block // rows, part] = total[
                :, part * width : (part + 1) * width
            ].reshape(block // rows, rows, width)


def opening(place, spectra, pick, put, keep, own, other, devices):
    order = keep.shape[0]
    rows = order // devices
    width = own[0].shape[1] // 2
    last = spectra.shape[3]
    held = list(own) + list(other)
    vmem = pl.BlockSpec(memory_space=pltpu.VMEM)
    return pl.pallas_call(
        functools.partial(opening_body, sources=len(held), scale=-1.0 / math.sqrt(order)),
        in_specs=[pl.BlockSpec(memory_space=pltpu.SMEM)]
        + [vmem] * 4
        + [pl.BlockSpec(memory_space=pl.ANY)] * len(held),
        out_specs=[vmem, vmem],
        out_shape=[
            jax.ShapeDtypeStruct((devices, 2, rows, width), jnp.bfloat16),
            jax.ShapeDtypeStruct((order, 2 * last), jnp.bfloat16),
        ],
        scratch_shapes=[pltpu.VMEM(array.shape, jnp.bfloat16) for array in held]
        + [
            pltpu.VMEM((2 * order, 2 * width), jnp.bfloat16),
            pltpu.SemaphoreType.DMA((len(held),)),
        ],
        compiler_params=pltpu.CompilerParams(vmem_limit_bytes=VMEM_LIMIT),
        cost_estimate=pl.CostEstimate(
            flops=16 * order * order * width, bytes_accessed=8 * order * order, transcendentals=0
        ),
        name="opening",
    )(place, spectra, pick, put, keep, *held)


def fill_tables(missing, neighbours, weights, order):
    shots = jnp.arange(order, dtype=jnp.int32)
    pick = jnp.zeros((missing.shape[0], order), jnp.float32)
    for slot in range(neighbours.shape[1]):
        pick = pick + jnp.where(
            neighbours[:, slot][:, None] == shots[None, :], weights[:, slot][:, None], 0.0
        )
    high = lax.reduce_precision(pick, 8, 7)
    found = shots[:, None] == missing[None, :]
    keep = 1.0 - jnp.any(found, axis=1, keepdims=True).astype(jnp.float32)
    both = jnp.concatenate([high, pick - high], axis=0).astype(jnp.bfloat16)
    return both, found.astype(jnp.bfloat16), keep


def spread(total, shares):
    widths = [total * share // PARTS for share in shares]
    return [(sum(widths[:index]), width) for index, width in enumerate(widths)]


def predict(records, missing, neighbours, weights, freq_bins):
    devices = lax.axis_size("shots")
    position = lax.axis_index("shots")
    shot_rows, order, samples = records.shape
    half = order // 2
    bins = freq_bins.shape[0]
    place_of = position.astype(jnp.int32).reshape(1)
    pairs = [(i, i ^ 1) for i in range(devices)]

    def exchange(blocks):
        return lax.all_to_all(blocks, "shots", split_axis=0, concat_axis=0, tiled=True)

    forward, inverse = tables(freq_bins, samples)
    pick, place, keep = fill_tables(missing, neighbours, weights, order)
    split = records.reshape(shot_rows, 2, half, samples)
    own, raw = [], []
    for first, width in spread(half, OUTWARD):
        block = forward_chunk(split, forward, first, width)
        block = exchange(block.reshape(devices, 2, shot_rows, width))
        raw.append(lax.ppermute(block, "shots", pairs))
        own.append(fill(block, pick, place, keep))
    other = [fill(block, pick, place, keep) for block in raw[:-1]]
    result = None
    for index, (first, width) in enumerate(spread(half, HOMEWARD)):
        loose = index == LOOSE and devices <= LOOSE_DEVICES
        if index == 0:
            block, filled = opening(place_of, raw[-1], pick, place, keep, own, other, devices)
            other = other + [filled]
        else:
            block = product(place_of, own, other, first, width, devices, loose)
        if loose:
            arrived = [block[0]]
            for step in range(1, devices):
                route = [(i, i ^ step) for i in range(devices)]
                arrived.append(lax.ppermute(block[step], "shots", route))
            result = loose_inverse(place_of, arrived, inverse, result, first)
        else:
            block = exchange(block)
            block = block.reshape(bins, 2, 2, shot_rows, width)
            result = inverse_chunk(block, inverse, result, first, half)
    return result.reshape(shot_rows, order, samples)


def solution(mesh):
    return jax.shard_map(
        predict,
        mesh=mesh,
        in_specs=(
            P(("lines", "shots"), None, None),
            P("lines"),
            P("lines", None),
            P("lines", None),
            P(),
        ),
        out_specs=P(("lines", "shots"), None, None),
        check_vma=False,
    )
```

```python
import functools
import math

import jax
import jax.numpy as jnp
from jax import lax
from jax.experimental import pallas as pl
from jax.experimental.pallas import tpu as pltpu
from jax.sharding import PartitionSpec as P


PARTS = 4
OUTWARD = (1, 3)
HOMEWARD = (1, 2, 1)
LOOSE_DEVICES = 16
CLOSING_VMEM = 62 * 1024 * 1024
OPENING_VMEM = 60 * 1024 * 1024
STREAM_VMEM = 36 * 1024 * 1024
VMEM_LIMIT = 24 * 1024 * 1024


def tables(freq_bins, sample_count):
    bin_count = freq_bins.shape[0]
    sample_ids = jnp.arange(sample_count, dtype=jnp.int32)
    phases = freq_bins[None, :] * sample_ids[:, None] % sample_count
    angles = phases.astype(jnp.float32) * (2.0 * math.pi / sample_count)
    trig_pair = jnp.stack([jnp.cos(angles), -jnp.sin(angles)], axis=-1)
    forward = (trig_pair / math.sqrt(sample_count)).astype(jnp.bfloat16)
    inverse = (trig_pair * math.sqrt(2.0 / bin_count)).astype(jnp.bfloat16)
    rows = lambda table: jnp.transpose(table, (1, 2, 0)).reshape(2 * bin_count, sample_count)
    return rows(forward), rows(inverse)


def shot_step(shot_rows):
    return math.gcd(shot_rows, 16)


def forward_body(
    records_ref, table_ref, out_ref, held_ref, rows_ref, sent_ref, semaphores, leaving, *, first
):
    pieces, step, width, samples = held_ref.shape
    planes = table_ref.shape[0]
    halves = records_ref.shape[1]
    places = [(shot * step, half) for shot in range(pieces // halves) for half in range(halves)]
    copies = [
        pltpu.make_async_copy(
            records_ref.at[pl.ds(shot, step), half, pl.ds(first, width), :],
            held_ref.at[piece],
            semaphores.at[piece],
        )
        for piece, (shot, half) in enumerate(places)
    ]
    for copy in copies:
        copy.start()
    for piece, (shot, half) in enumerate(places):
        copies[piece].wait()
        spectra = lax.dot_general(
            table_ref[...],
            held_ref[piece].reshape(step * width, samples),
            (((1,), (1,)), ((), ())),
            preferred_element_type=jnp.float32,
        )
        for row in range(step):
            rows_ref[:, row, :] = spectra[:, row * width : (row + 1) * width]
        sent_ref[piece] = rows_ref[...].astype(jnp.bfloat16).reshape(planes // 2, 2, step, width)
        copies[piece] = pltpu.make_async_copy(
            sent_ref.at[piece],
            out_ref.at[:, half, :, pl.ds(shot, step), :],
            leaving.at[piece],
        )
        copies[piece].start()
    for copy in copies:
        copy.wait()


def forward_chunk(records, table, first, width):
    shot_rows, halves, _, samples = records.shape
    planes = table.shape[0]
    step = shot_step(shot_rows)
    pieces = halves * shot_rows // step
    vmem = pl.BlockSpec(memory_space=pltpu.VMEM)
    return pl.pallas_call(
        functools.partial(forward_body, first=first),
        in_specs=[pl.BlockSpec(memory_space=pl.ANY), vmem],
        out_specs=pl.BlockSpec(memory_space=pl.ANY),
        out_shape=jax.ShapeDtypeStruct((planes // 2, halves, 2, shot_rows, width), jnp.bfloat16),
        scratch_shapes=[
            pltpu.VMEM((pieces, step, width, samples), jnp.bfloat16),
            pltpu.VMEM((planes, step, width), jnp.float32),
            pltpu.VMEM((pieces, planes // 2, 2, step, width), jnp.bfloat16),
            pltpu.SemaphoreType.DMA((pieces,)),
            pltpu.SemaphoreType.DMA((pieces,)),
        ],
        compiler_params=pltpu.CompilerParams(vmem_limit_bytes=STREAM_VMEM),
        cost_estimate=pl.CostEstimate(
            flops=2 * shot_rows * halves * width * samples * planes,
            bytes_accessed=2 * shot_rows * halves * width * samples,
            transcendentals=0,
        ),
    )(records, table)


def inverse_body(planes_ref, table_ref, *refs, first):
    out_ref, held_ref, rows_ref, semaphores = refs[-4:]
    bins, halves, parts, _, width = planes_ref.shape
    pieces, step = held_ref.shape[:2]
    copies = []
    for piece in range(pieces):
        shot, half = piece // halves * step, piece % halves
        rows_ref[...] = (
            planes_ref[:, half, :, shot : shot + step, :]
            .astype(jnp.float32)
            .reshape(bins * parts, step, width)
        )
        for row in range(step):
            left = rows_ref[:, row, :].astype(jnp.bfloat16)
            held_ref[piece, row] = lax.dot_general(
                left, table_ref[...], (((0,), (0,)), ((), ())), preferred_element_type=jnp.float32
            ).astype(jnp.bfloat16)
        copy = pltpu.make_async_copy(
            held_ref.at[piece],
            out_ref.at[pl.ds(shot, step), half, pl.ds(first, width), :],
            semaphores.at[piece],
        )
        copy.start()
        copies.append(copy)
    for copy in copies:
        copy.wait()


def inverse_chunk(returned, table, kept, first, half):
    _, halves, _, shot_rows, width = returned.shape
    planes, samples = table.shape
    step = shot_step(shot_rows)
    pieces = halves * shot_rows // step
    vmem = pl.BlockSpec(memory_space=pltpu.VMEM)
    operands = [returned, table] + ([] if kept is None else [kept])
    return pl.pallas_call(
        functools.partial(inverse_body, first=first),
        in_specs=[vmem, vmem] + [pl.BlockSpec(memory_space=pl.ANY)] * (len(operands) - 2),
        out_specs=pl.BlockSpec(memory_space=pl.ANY),
        out_shape=jax.ShapeDtypeStruct((shot_rows, halves, half, samples), jnp.bfloat16),
        scratch_shapes=[
            pltpu.VMEM((pieces, step, width, samples), jnp.bfloat16),
            pltpu.VMEM((planes, step, width), jnp.float32),
            pltpu.SemaphoreType.DMA((pieces,)),
        ],
        input_output_aliases={} if kept is None else {2: 0},
        compiler_params=pltpu.CompilerParams(vmem_limit_bytes=STREAM_VMEM),
        cost_estimate=pl.CostEstimate(
            flops=2 * shot_rows * halves * width * samples * planes,
            bytes_accessed=2 * shot_rows * halves * width * samples,
            transcendentals=0,
        ),
    )(*operands)


def loose_body(place_ref, table_ref, kept_ref, *refs, first):
    pieces_refs, (out_ref, held_ref, planes_ref, semaphores) = refs[:-4], refs[-4:]
    pieces, step = held_ref.shape[:2]
    halves = out_ref.shape[1]
    position = place_ref[0]
    for index, piece_ref in enumerate(pieces_refs):
        source = jnp.bitwise_xor(position, index)
        for part in range(piece_ref.shape[0]):
            planes_ref[source % 2, source // 2 * 2 + part] = piece_ref[part].astype(jnp.float32)
    copies = []
    for piece in range(pieces):
        shot, half = piece // halves * step, piece % halves
        for row in range(step):
            left = planes_ref[half, :, shot + row, :].astype(jnp.bfloat16)
            held_ref[piece, row] = lax.dot_general(
                left, table_ref[...], (((0,), (0,)), ((), ())), preferred_element_type=jnp.float32
            ).astype(jnp.bfloat16)
        copy = pltpu.make_async_copy(
            held_ref.at[piece],
            out_ref.at[pl.ds(shot, step), half, pl.ds(first, held_ref.shape[2]), :],
            semaphores.at[piece],
        )
        copy.start()
        copies.append(copy)
    for copy in copies:
        copy.wait()


def loose_inverse(place, returned, table, kept, first):
    _, shot_rows, width = returned[0].shape
    halves = kept.shape[1]
    planes, samples = table.shape
    step = shot_step(shot_rows)
    pieces = halves * shot_rows // step
    vmem = pl.BlockSpec(memory_space=pltpu.VMEM)
    anywhere = pl.BlockSpec(memory_space=pl.ANY)
    return pl.pallas_call(
        functools.partial(loose_body, first=first),
        in_specs=[pl.BlockSpec(memory_space=pltpu.SMEM), vmem, anywhere] + [vmem] * len(returned),
        out_specs=anywhere,
        out_shape=jax.ShapeDtypeStruct(kept.shape, kept.dtype),
        scratch_shapes=[
            pltpu.VMEM((pieces, step, width, samples), jnp.bfloat16),
            pltpu.VMEM((halves, planes, shot_rows, width), jnp.float32),
            pltpu.SemaphoreType.DMA((pieces,)),
        ],
        input_output_aliases={2: 0},
        compiler_params=pltpu.CompilerParams(vmem_limit_bytes=STREAM_VMEM),
        cost_estimate=pl.CostEstimate(
            flops=2 * shot_rows * halves * width * samples * planes,
            bytes_accessed=2 * shot_rows * halves * width * samples,
            transcendentals=0,
        ),
    )(place, table, kept, *returned)


def fill_into(out_ref, spectra_ref, pick_ref, put_ref, keep_ref):
    devices, parts, rows, width = spectra_ref.shape
    count = pick_ref.shape[0] // 2
    for part in range(parts):
        recorded = spectra_ref[:, part].reshape(devices * rows, width)
        both = jnp.dot(pick_ref[...], recorded, preferred_element_type=jnp.float32)
        replaced = (both[:count] + both[count:]).astype(jnp.bfloat16)
        placed = jnp.dot(put_ref[...], replaced, preferred_element_type=jnp.float32)
        out_ref[:, part * width : (part + 1) * width] = placed.astype(jnp.bfloat16) + recorded * keep_ref[
            ...
        ].astype(jnp.bfloat16)


def fill_body(spectra_ref, pick_ref, put_ref, keep_ref, out_ref):
    fill_into(out_ref, spectra_ref, pick_ref, put_ref, keep_ref)


def fill(spectra, pick, place, keep):
    devices, parts, rows, width = spectra.shape
    order = devices * rows
    return pl.pallas_call(
        fill_body,
        out_shape=jax.ShapeDtypeStruct((order, parts * width), jnp.bfloat16),
        compiler_params=pltpu.CompilerParams(vmem_limit_bytes=VMEM_LIMIT),
        cost_estimate=pl.CostEstimate(
            flops=8 * pick.shape[0] * order * width,
            bytes_accessed=8 * order * width,
            transcendentals=0,
        ),
        name="fill",
    )(spectra, pick, place, keep)


def closing_body(place_ref, *refs, sources, middle, scale):
    source_refs, refs = refs[:sources], refs[sources:]
    held_refs, (right_ref, total_ref, semaphores) = refs[-sources - 3 : -3], refs[-3:]
    out_refs = refs[: -sources - 3]
    count = sources // 2
    column_ref = held_refs[count - 1]
    order = column_ref.shape[0]
    half = order // 2
    width = column_ref.shape[1] // 2
    position = place_ref[0]
    member = position % 2
    copies = [
        pltpu.make_async_copy(source, held, semaphores.at[index])
        for index, (source, held) in enumerate(zip(source_refs, held_refs))
    ]
    for index in [count - 1] + [index for index in range(sources) if index != count - 1]:
        copies[index].start()
    copies[count - 1].wait()
    line = 0
    for index, left in enumerate(held_refs):
        if index % count == 0:
            start = (member if index == 0 else 1 - member) * half
        depth = left.shape[1] // 2
        lines = pl.ds(pl.multiple_of(start, 128), depth)
        real = column_ref[lines, :width]
        imag = column_ref[lines, width:]
        right_ref[line : line + depth, :width] = real
        right_ref[line : line + depth, width:] = imag
        right_ref[line + depth : line + 2 * depth, :width] = -imag
        right_ref[line + depth : line + 2 * depth, width:] = real
        line += 2 * depth
        start += depth
    for index in range(sources):
        if index != count - 1:
            copies[index].wait()
    block = math.gcd(order, 512)
    for row in range(0, order, block):
        total = None
        line = 0
        for left in held_refs:
            depth = left.shape[1]
            term = jnp.dot(
                left[row : row + block], right_ref[line : line + depth], preferred_element_type=jnp.float32
            )
            total = term if total is None else total + term
            line += depth
        total_ref[row : row + block] = (total * scale).astype(jnp.bfloat16)
    last_ref = out_refs[-1]
    devices, parts, rows, _ = last_ref.shape
    for part in range(parts):
        begin = part * width
        last_ref[:, part] = total_ref[:, begin + middle : begin + width].reshape(
            devices, rows, width - middle
        )
        if len(out_refs) == 2:
            out_refs[0][:, part] = total_ref[:, begin : begin + middle].reshape(devices, rows, middle)
            continue
        for index, out_ref in enumerate(out_refs[:-1]):
            target = jnp.bitwise_xor(position, index)
            lines = pl.ds(pl.multiple_of(target * rows, rows), rows)
            out_ref[part] = total_ref[lines, begin : begin + middle]


def closing(place, own, other, middle, devices, loose):
    order, columns = own[-1].shape
    rows = order // devices
    width = columns // 2
    held = list(own) + list(other)
    vmem = pl.BlockSpec(memory_space=pltpu.VMEM)
    blocks = lambda size: jax.ShapeDtypeStruct((devices, 2, rows, size), jnp.bfloat16)
    shapes = [blocks(middle)]
    if loose:
        shapes = [jax.ShapeDtypeStruct((2, rows, middle), jnp.bfloat16)] * devices
    shapes = shapes + [blocks(width - middle)]
    return pl.pallas_call(
        functools.partial(
            closing_body, sources=len(held), middle=middle, scale=-1.0 / math.sqrt(order)
        ),
        in_specs=[pl.BlockSpec(memory_space=pltpu.SMEM)]
        + [pl.BlockSpec(memory_space=pl.ANY)] * len(held),
        out_specs=[vmem] * len(shapes),
        out_shape=shapes,
        scratch_shapes=[pltpu.VMEM(array.shape, jnp.bfloat16) for array in held]
        + [
            pltpu.VMEM((2 * order, columns), jnp.bfloat16),
            pltpu.VMEM((order, columns), jnp.bfloat16),
            pltpu.SemaphoreType.DMA((len(held),)),
        ],
        compiler_params=pltpu.CompilerParams(vmem_limit_bytes=CLOSING_VMEM),
        cost_estimate=pl.CostEstimate(
            flops=16 * order * order * width, bytes_accessed=8 * order * order, transcendentals=0
        ),
        name="closing",
    )(place, *held)


def opening_body(place_ref, spectra_ref, pick_ref, put_ref, keep_ref, *refs, sources, scale):
    source_refs, refs = refs[:sources], refs[sources:]
    out_ref, filled_out = refs[:2]
    held_refs, (filled_ref, sent_ref, right_ref, semaphores, leaving) = refs[2:-5], refs[-5:]
    copies = [
        pltpu.make_async_copy(source, held, semaphores.at[index])
        for index, (source, held) in enumerate(zip(source_refs, held_refs))
    ]
    for copy in copies:
        copy.start()
    fill_into(filled_ref, spectra_ref, pick_ref, put_ref, keep_ref)
    departures = [pltpu.make_async_copy(filled_ref, filled_out, leaving.at[0])]
    departures[0].start()
    for copy in copies:
        copy.wait()
    order = filled_ref.shape[0]
    half = order // 2
    _, parts, rows, width = out_ref.shape
    count = (sources + 1) // 2
    lefts = list(held_refs) + [filled_ref]
    own_ref = held_refs[0]
    member = place_ref[0] % 2
    line = 0
    for index, left in enumerate(lefts):
        if index % count == 0:
            start = (member if index == 0 else 1 - member) * half
        depth = left.shape[1] // 2
        lines = pl.ds(pl.multiple_of(start, 128), depth)
        real = own_ref[lines, :width]
        imag = own_ref[lines, width:]
        right_ref[line : line + depth, :width] = real
        right_ref[line : line + depth, width:] = imag
        right_ref[line + depth : line + 2 * depth, :width] = -imag
        right_ref[line + depth : line + 2 * depth, width:] = real
        line += 2 * depth
        start += depth
    block = math.gcd(order, 256)
    for row in range(0, order, block):
        total = None
        line = 0
        for left in lefts:
            depth = left.shape[1]
            term = jnp.dot(
                left[row : row + block], right_ref[line : line + depth], preferred_element_type=jnp.float32
            )
            total = term if total is None else total + term
            line += depth
        total = (total * scale).astype(jnp.bfloat16)
        first = row // rows
        for part in range(parts):
            sent_ref[first : first + block // rows, part] = total[
                :, part * width : (part + 1) * width
            ].reshape(block // rows, rows, width)
        span = pl.ds(first, block // rows)
        departures.append(
            pltpu.make_async_copy(sent_ref.at[span], out_ref.at[span], leaving.at[1 + row // block])
        )
        departures[-1].start()
    for copy in departures:
        copy.wait()


def opening(place, spectra, pick, put, keep, own, other, devices):
    order = keep.shape[0]
    rows = order // devices
    width = own[0].shape[1] // 2
    last = spectra.shape[3]
    held = list(own) + list(other)
    vmem = pl.BlockSpec(memory_space=pltpu.VMEM)
    return pl.pallas_call(
        functools.partial(opening_body, sources=len(held), scale=-1.0 / math.sqrt(order)),
        in_specs=[pl.BlockSpec(memory_space=pltpu.SMEM)]
        + [vmem] * 4
        + [pl.BlockSpec(memory_space=pl.ANY)] * len(held),
        out_specs=[pl.BlockSpec(memory_space=pl.ANY)] * 2,
        out_shape=[
            jax.ShapeDtypeStruct((devices, 2, rows, width), jnp.bfloat16),
            jax.ShapeDtypeStruct((order, 2 * last), jnp.bfloat16),
        ],
        scratch_shapes=[pltpu.VMEM(array.shape, jnp.bfloat16) for array in held]
        + [
            pltpu.VMEM((order, 2 * last), jnp.bfloat16),
            pltpu.VMEM((devices, 2, rows, width), jnp.bfloat16),
            pltpu.VMEM((2 * order, 2 * width), jnp.bfloat16),
            pltpu.SemaphoreType.DMA((len(held),)),
            pltpu.SemaphoreType.DMA((1 + order // math.gcd(order, 256),)),
        ],
        compiler_params=pltpu.CompilerParams(vmem_limit_bytes=OPENING_VMEM),
        cost_estimate=pl.CostEstimate(
            flops=16 * order * order * width, bytes_accessed=8 * order * order, transcendentals=0
        ),
        name="opening",
    )(place, spectra, pick, put, keep, *held)


def fill_tables(missing, neighbours, weights, order):
    shots = jnp.arange(order, dtype=jnp.int32)
    pick = jnp.zeros((missing.shape[0], order), jnp.float32)
    for slot in range(neighbours.shape[1]):
        pick = pick + jnp.where(
            neighbours[:, slot][:, None] == shots[None, :], weights[:, slot][:, None], 0.0
        )
    high = lax.reduce_precision(pick, 8, 7)
    found = shots[:, None] == missing[None, :]
    keep = 1.0 - jnp.any(found, axis=1, keepdims=True).astype(jnp.float32)
    both = jnp.concatenate([high, pick - high], axis=0).astype(jnp.bfloat16)
    return both, found.astype(jnp.bfloat16), keep


def spread(total, shares):
    widths = [total * share // PARTS for share in shares]
    return [(sum(widths[:index]), width) for index, width in enumerate(widths)]


def predict(records, missing, neighbours, weights, freq_bins):
    devices = lax.axis_size("shots")
    position = lax.axis_index("shots")
    shot_rows, order, samples = records.shape
    half = order // 2
    bins = freq_bins.shape[0]
    place_of = position.astype(jnp.int32).reshape(1)
    pairs = [(i, i ^ 1) for i in range(devices)]

    def exchange(blocks):
        return lax.all_to_all(blocks, "shots", split_axis=0, concat_axis=0, tiled=True)

    forward, inverse = tables(freq_bins, samples)
    pick, place, keep = fill_tables(missing, neighbours, weights, order)
    split = records.reshape(shot_rows, 2, half, samples)
    own, raw = [], []
    for first, width in spread(half, OUTWARD):
        block = forward_chunk(split, forward, first, width)
        block = exchange(block.reshape(devices, 2, shot_rows, width))
        raw.append(lax.ppermute(block, "shots", pairs))
        own.append(fill(block, pick, place, keep))
    other = [fill(block, pick, place, keep) for block in raw[:-1]]
    mixed = devices <= LOOSE_DEVICES
    homeward = spread(half, HOMEWARD)
    result = None
    for index, (first, width) in enumerate(homeward):
        if index != 2:
            if index == 0:
                block, filled = opening(place_of, raw[-1], pick, place, keep, own, other, devices)
                other = other + [filled]
            else:
                *blocks, final = closing(place_of, own, other, width, devices, mixed)
                block = blocks[0]
        else:
            block = final
        if index == 1 and mixed:
            arrived = [block]
            for step in range(1, devices):
                route = [(i, i ^ step) for i in range(devices)]
                arrived.append(lax.ppermute(blocks[step], "shots", route))
            result = loose_inverse(place_of, arrived, inverse, result, first)
        else:
            block = exchange(block)
            block = block.reshape(bins, 2, 2, shot_rows, width)
            result = inverse_chunk(block, inverse, result, first, half)
    return result.reshape(shot_rows, order, samples)


def solution(mesh):
    return jax.shard_map(
        predict,
        mesh=mesh,
        in_specs=(
            P(("lines", "shots"), None, None),
            P("lines"),
            P("lines", None),
            P("lines", None),
            P(),
        ),
        out_specs=P(("lines", "shots"), None, None),
        check_vma=False,
    )
```

```python
import functools
import math

import jax
import jax.numpy as jnp
from jax import lax
from jax.experimental import pallas as pl
from jax.experimental.pallas import tpu as pltpu
from jax.sharding import PartitionSpec as P


PARTS = 4
OUTWARD = (1, 3)
HOMEWARD = (1, 2, 1)
LOOSE_DEVICES = 16
CLOSING_VMEM = 62 * 1024 * 1024
OPENING_VMEM = 60 * 1024 * 1024
STREAM_VMEM = 36 * 1024 * 1024
VMEM_LIMIT = 24 * 1024 * 1024


def tables(freq_bins, sample_count):
    bin_count = freq_bins.shape[0]
    sample_ids = jnp.arange(sample_count, dtype=jnp.int32)
    phases = freq_bins[None, :] * sample_ids[:, None] % sample_count
    angles = phases.astype(jnp.float32) * (2.0 * math.pi / sample_count)
    trig_pair = jnp.stack([jnp.cos(angles), -jnp.sin(angles)], axis=-1)
    forward = (trig_pair / math.sqrt(sample_count)).astype(jnp.bfloat16)
    inverse = (trig_pair * math.sqrt(2.0 / bin_count)).astype(jnp.bfloat16)
    rows = lambda table: jnp.transpose(table, (1, 2, 0)).reshape(2 * bin_count, sample_count)
    return rows(forward), rows(inverse)


def shot_step(shot_rows):
    return math.gcd(shot_rows, 16)


def forward_body(
    records_ref, table_ref, out_ref, held_ref, rows_ref, sent_ref, semaphores, leaving, *, first
):
    pieces, step, width, samples = held_ref.shape
    planes = table_ref.shape[0]
    halves = records_ref.shape[1]
    places = [(shot * step, half) for shot in range(pieces // halves) for half in range(halves)]
    copies = [
        pltpu.make_async_copy(
            records_ref.at[pl.ds(shot, step), half, pl.ds(first, width), :],
            held_ref.at[piece],
            semaphores.at[piece],
        )
        for piece, (shot, half) in enumerate(places)
    ]
    for copy in copies:
        copy.start()
    for piece, (shot, half) in enumerate(places):
        copies[piece].wait()
        spectra = lax.dot_general(
            table_ref[...],
            held_ref[piece].reshape(step * width, samples),
            (((1,), (1,)), ((), ())),
            preferred_element_type=jnp.float32,
        )
        for row in range(step):
            rows_ref[:, row, :] = spectra[:, row * width : (row + 1) * width]
        sent_ref[piece] = rows_ref[...].astype(jnp.bfloat16).reshape(planes // 2, 2, step, width)
        copies[piece] = pltpu.make_async_copy(
            sent_ref.at[piece],
            out_ref.at[:, half, :, pl.ds(shot, step), :],
            leaving.at[piece],
        )
        copies[piece].start()
    for copy in copies:
        copy.wait()


def forward_chunk(records, table, first, width):
    shot_rows, halves, _, samples = records.shape
    planes = table.shape[0]
    step = shot_step(shot_rows)
    pieces = halves * shot_rows // step
    vmem = pl.BlockSpec(memory_space=pltpu.VMEM)
    return pl.pallas_call(
        functools.partial(forward_body, first=first),
        in_specs=[pl.BlockSpec(memory_space=pl.ANY), vmem],
        out_specs=pl.BlockSpec(memory_space=pl.ANY),
        out_shape=jax.ShapeDtypeStruct((planes // 2, halves, 2, shot_rows, width), jnp.bfloat16),
        scratch_shapes=[
            pltpu.VMEM((pieces, step, width, samples), jnp.bfloat16),
            pltpu.VMEM((planes, step, width), jnp.float32),
            pltpu.VMEM((pieces, planes // 2, 2, step, width), jnp.bfloat16),
            pltpu.SemaphoreType.DMA((pieces,)),
            pltpu.SemaphoreType.DMA((pieces,)),
        ],
        compiler_params=pltpu.CompilerParams(vmem_limit_bytes=STREAM_VMEM),
        cost_estimate=pl.CostEstimate(
            flops=2 * shot_rows * halves * width * samples * planes,
            bytes_accessed=2 * shot_rows * halves * width * samples,
            transcendentals=0,
        ),
    )(records, table)


def inverse_body(planes_ref, table_ref, *refs, first):
    out_ref, held_ref, rows_ref, semaphores = refs[-4:]
    bins, halves, parts, _, width = planes_ref.shape
    pieces, step = held_ref.shape[:2]
    copies = []
    for piece in range(pieces):
        shot, half = piece // halves * step, piece % halves
        rows_ref[...] = (
            planes_ref[:, half, :, shot : shot + step, :]
            .astype(jnp.float32)
            .reshape(bins * parts, step, width)
        )
        for row in range(step):
            left = rows_ref[:, row, :].astype(jnp.bfloat16)
            held_ref[piece, row] = lax.dot_general(
                left, table_ref[...], (((0,), (0,)), ((), ())), preferred_element_type=jnp.float32
            ).astype(jnp.bfloat16)
        copy = pltpu.make_async_copy(
            held_ref.at[piece],
            out_ref.at[pl.ds(shot, step), half, pl.ds(first, width), :],
            semaphores.at[piece],
        )
        copy.start()
        copies.append(copy)
    for copy in copies:
        copy.wait()


def inverse_chunk(returned, table, kept, first, half):
    _, halves, _, shot_rows, width = returned.shape
    planes, samples = table.shape
    step = shot_step(shot_rows)
    pieces = halves * shot_rows // step
    vmem = pl.BlockSpec(memory_space=pltpu.VMEM)
    operands = [returned, table] + ([] if kept is None else [kept])
    return pl.pallas_call(
        functools.partial(inverse_body, first=first),
        in_specs=[vmem, vmem] + [pl.BlockSpec(memory_space=pl.ANY)] * (len(operands) - 2),
        out_specs=pl.BlockSpec(memory_space=pl.ANY),
        out_shape=jax.ShapeDtypeStruct((shot_rows, halves, half, samples), jnp.bfloat16),
        scratch_shapes=[
            pltpu.VMEM((pieces, step, width, samples), jnp.bfloat16),
            pltpu.VMEM((planes, step, width), jnp.float32),
            pltpu.SemaphoreType.DMA((pieces,)),
        ],
        input_output_aliases={} if kept is None else {2: 0},
        compiler_params=pltpu.CompilerParams(vmem_limit_bytes=STREAM_VMEM),
        cost_estimate=pl.CostEstimate(
            flops=2 * shot_rows * halves * width * samples * planes,
            bytes_accessed=2 * shot_rows * halves * width * samples,
            transcendentals=0,
        ),
    )(*operands)


def loose_body(place_ref, table_ref, kept_ref, *refs, first):
    pieces_refs, (out_ref, held_ref, planes_ref, semaphores) = refs[:-4], refs[-4:]
    pieces, step = held_ref.shape[:2]
    halves = out_ref.shape[1]
    position = place_ref[0]
    for index, piece_ref in enumerate(pieces_refs):
        source = jnp.bitwise_xor(position, index)
        for part in range(piece_ref.shape[0]):
            planes_ref[source % 2, source // 2 * 2 + part] = piece_ref[part].astype(jnp.float32)
    copies = []
    for piece in range(pieces):
        shot, half = piece // halves * step, piece % halves
        for row in range(step):
            left = planes_ref[half, :, shot + row, :].astype(jnp.bfloat16)
            held_ref[piece, row] = lax.dot_general(
                left, table_ref[...], (((0,), (0,)), ((), ())), preferred_element_type=jnp.float32
            ).astype(jnp.bfloat16)
        copy = pltpu.make_async_copy(
            held_ref.at[piece],
            out_ref.at[pl.ds(shot, step), half, pl.ds(first, held_ref.shape[2]), :],
            semaphores.at[piece],
        )
        copy.start()
        copies.append(copy)
    for copy in copies:
        copy.wait()


def loose_inverse(place, returned, table, kept, first):
    _, shot_rows, width = returned[0].shape
    halves = kept.shape[1]
    planes, samples = table.shape
    step = shot_step(shot_rows)
    pieces = halves * shot_rows // step
    vmem = pl.BlockSpec(memory_space=pltpu.VMEM)
    anywhere = pl.BlockSpec(memory_space=pl.ANY)
    return pl.pallas_call(
        functools.partial(loose_body, first=first),
        in_specs=[pl.BlockSpec(memory_space=pltpu.SMEM), vmem, anywhere] + [vmem] * len(returned),
        out_specs=anywhere,
        out_shape=jax.ShapeDtypeStruct(kept.shape, kept.dtype),
        scratch_shapes=[
            pltpu.VMEM((pieces, step, width, samples), jnp.bfloat16),
            pltpu.VMEM((halves, planes, shot_rows, width), jnp.float32),
            pltpu.SemaphoreType.DMA((pieces,)),
        ],
        input_output_aliases={2: 0},
        compiler_params=pltpu.CompilerParams(vmem_limit_bytes=STREAM_VMEM),
        cost_estimate=pl.CostEstimate(
            flops=2 * shot_rows * halves * width * samples * planes,
            bytes_accessed=2 * shot_rows * halves * width * samples,
            transcendentals=0,
        ),
    )(place, table, kept, *returned)


def fill_into(out_ref, spectra_ref, pick_ref, put_ref, keep_ref):
    devices, parts, rows, width = spectra_ref.shape
    count = pick_ref.shape[0] // 2
    for part in range(parts):
        recorded = spectra_ref[:, part].reshape(devices * rows, width)
        both = jnp.dot(pick_ref[...], recorded, preferred_element_type=jnp.float32)
        replaced = (both[:count] + both[count:]).astype(jnp.bfloat16)
        placed = jnp.dot(put_ref[...], replaced, preferred_element_type=jnp.float32)
        out_ref[:, part * width : (part + 1) * width] = placed.astype(jnp.bfloat16) + recorded * keep_ref[
            ...
        ].astype(jnp.bfloat16)


def fill_body(spectra_ref, pick_ref, put_ref, keep_ref, out_ref):
    fill_into(out_ref, spectra_ref, pick_ref, put_ref, keep_ref)


def fill(spectra, pick, place, keep):
    devices, parts, rows, width = spectra.shape
    order = devices * rows
    return pl.pallas_call(
        fill_body,
        out_shape=jax.ShapeDtypeStruct((order, parts * width), jnp.bfloat16),
        compiler_params=pltpu.CompilerParams(vmem_limit_bytes=VMEM_LIMIT),
        cost_estimate=pl.CostEstimate(
            flops=8 * pick.shape[0] * order * width,
            bytes_accessed=8 * order * width,
            transcendentals=0,
        ),
        name="fill",
    )(spectra, pick, place, keep)


def closing_body(place_ref, *refs, sources, middle, scale):
    source_refs, refs = refs[:sources], refs[sources:]
    held_refs, (right_ref, total_ref, semaphores) = refs[-sources - 3 : -3], refs[-3:]
    out_refs = refs[: -sources - 3]
    count = sources // 2
    column_ref = held_refs[count - 1]
    order = column_ref.shape[0]
    half = order // 2
    width = column_ref.shape[1] // 2
    position = place_ref[0]
    member = position % 2
    copies = [
        pltpu.make_async_copy(source, held, semaphores.at[index])
        for index, (source, held) in enumerate(zip(source_refs, held_refs))
    ]
    for index in [count - 1] + [index for index in range(sources) if index != count - 1]:
        copies[index].start()
    copies[count - 1].wait()
    line = 0
    for index, left in enumerate(held_refs):
        if index % count == 0:
            start = (member if index == 0 else 1 - member) * half
        depth = left.shape[1] // 2
        lines = pl.ds(pl.multiple_of(start, 128), depth)
        real = column_ref[lines, :width]
        imag = column_ref[lines, width:]
        right_ref[line : line + depth, :width] = real
        right_ref[line : line + depth, width:] = imag
        right_ref[line + depth : line + 2 * depth, :width] = -imag
        right_ref[line + depth : line + 2 * depth, width:] = real
        line += 2 * depth
        start += depth
    for index in range(sources):
        if index != count - 1:
            copies[index].wait()
    block = math.gcd(order, 512)
    for row in range(0, order, block):
        total = None
        line = 0
        for left in held_refs:
            depth = left.shape[1]
            term = jnp.dot(
                left[row : row + block], right_ref[line : line + depth], preferred_element_type=jnp.float32
            )
            total = term if total is None else total + term
            line += depth
        total_ref[row : row + block] = (total * scale).astype(jnp.bfloat16)
    last_ref = out_refs[-1]
    devices, parts, rows, _ = last_ref.shape
    for part in range(parts):
        begin = part * width
        last_ref[:, part] = total_ref[:, begin + middle : begin + width].reshape(
            devices, rows, width - middle
        )
        if len(out_refs) == 2:
            out_refs[0][:, part] = total_ref[:, begin : begin + middle].reshape(devices, rows, middle)
            continue
        for index, out_ref in enumerate(out_refs[:-1]):
            target = jnp.bitwise_xor(position, index)
            lines = pl.ds(pl.multiple_of(target * rows, rows), rows)
            out_ref[part] = total_ref[lines, begin : begin + middle]


def closing(place, own, other, middle, devices, loose):
    order, columns = own[-1].shape
    rows = order // devices
    width = columns // 2
    held = list(own) + list(other)
    vmem = pl.BlockSpec(memory_space=pltpu.VMEM)
    blocks = lambda size: jax.ShapeDtypeStruct((devices, 2, rows, size), jnp.bfloat16)
    shapes = [blocks(middle)]
    if loose:
        shapes = [jax.ShapeDtypeStruct((2, rows, middle), jnp.bfloat16)] * devices
    shapes = shapes + [blocks(width - middle)]
    return pl.pallas_call(
        functools.partial(
            closing_body, sources=len(held), middle=middle, scale=-1.0 / math.sqrt(order)
        ),
        in_specs=[pl.BlockSpec(memory_space=pltpu.SMEM)]
        + [pl.BlockSpec(memory_space=pl.ANY)] * len(held),
        out_specs=[vmem] * len(shapes),
        out_shape=shapes,
        scratch_shapes=[pltpu.VMEM(array.shape, jnp.bfloat16) for array in held]
        + [
            pltpu.VMEM((2 * order, columns), jnp.bfloat16),
            pltpu.VMEM((order, columns), jnp.bfloat16),
            pltpu.SemaphoreType.DMA((len(held),)),
        ],
        compiler_params=pltpu.CompilerParams(vmem_limit_bytes=CLOSING_VMEM),
        cost_estimate=pl.CostEstimate(
            flops=16 * order * order * width, bytes_accessed=8 * order * order, transcendentals=0
        ),
        name="closing",
    )(place, *held)


def fill_right(right_ref, own_ref, depths, start):
    width = own_ref.shape[1] // 2
    line = 0
    for depth in depths:
        lines = pl.ds(pl.multiple_of(start, 128), depth)
        real = own_ref[lines, :width]
        imag = own_ref[lines, width:]
        right_ref[line : line + depth, :width] = real
        right_ref[line : line + depth, width:] = imag
        right_ref[line + depth : line + 2 * depth, :width] = -imag
        right_ref[line + depth : line + 2 * depth, width:] = real
        line += 2 * depth
        start += depth


def early_body(place_ref, one_ref, two_ref, out_ref, right_ref):
    order = out_ref.shape[0]
    depths = [one_ref.shape[1] // 2, two_ref.shape[1] // 2]
    fill_right(right_ref, one_ref, depths, place_ref[0] % 2 * (order // 2))
    cut = 2 * depths[0]
    block = math.gcd(order, 256)
    for row in range(0, order, block):
        out_ref[row : row + block] = jnp.dot(
            one_ref[row : row + block], right_ref[:cut], preferred_element_type=jnp.float32
        ) + jnp.dot(two_ref[row : row + block], right_ref[cut:], preferred_element_type=jnp.float32)


def early(place, one, two):
    order, columns = one.shape
    vmem = pl.BlockSpec(memory_space=pltpu.VMEM)
    return pl.pallas_call(
        early_body,
        in_specs=[pl.BlockSpec(memory_space=pltpu.SMEM), vmem, vmem],
        out_specs=vmem,
        out_shape=jax.ShapeDtypeStruct((order, columns), jnp.float32),
        scratch_shapes=[pltpu.VMEM((order, columns), jnp.bfloat16)],
        compiler_params=pltpu.CompilerParams(vmem_limit_bytes=VMEM_LIMIT),
        cost_estimate=pl.CostEstimate(
            flops=2 * order * order * columns, bytes_accessed=4 * order * order, transcendentals=0
        ),
        name="early",
    )(place, one, two)


def opening_body(place_ref, spectra_ref, pick_ref, put_ref, keep_ref, grown_ref, *refs, sources, scale):
    source_refs, refs = refs[:sources], refs[sources:]
    out_ref, filled_out = refs[:2]
    held_refs, (filled_ref, sent_ref, right_ref, semaphores, leaving) = refs[2:-5], refs[-5:]
    copies = [
        pltpu.make_async_copy(source, held, semaphores.at[index])
        for index, (source, held) in enumerate(zip(source_refs, held_refs))
    ]
    for copy in copies:
        copy.start()
    fill_into(filled_ref, spectra_ref, pick_ref, put_ref, keep_ref)
    departures = [pltpu.make_async_copy(filled_ref, filled_out, leaving.at[0])]
    departures[0].start()
    for copy in copies:
        copy.wait()
    order = filled_ref.shape[0]
    half = order // 2
    _, parts, rows, width = out_ref.shape
    own_ref = held_refs[0]
    lefts = [held_refs[1], filled_ref]
    fill_right(right_ref, own_ref, [left.shape[1] // 2 for left in lefts], (1 - place_ref[0] % 2) * half)
    block = math.gcd(order, 256)
    for row in range(0, order, block):
        total = grown_ref[row : row + block]
        line = 0
        for left in lefts:
            depth = left.shape[1]
            term = jnp.dot(
                left[row : row + block], right_ref[line : line + depth], preferred_element_type=jnp.float32
            )
            total = total + term
            line += depth
        total = (total * scale).astype(jnp.bfloat16)
        first = row // rows
        for part in range(parts):
            sent_ref[first : first + block // rows, part] = total[
                :, part * width : (part + 1) * width
            ].reshape(block // rows, rows, width)
        span = pl.ds(first, block // rows)
        departures.append(
            pltpu.make_async_copy(sent_ref.at[span], out_ref.at[span], leaving.at[1 + row // block])
        )
        departures[-1].start()
    for copy in departures:
        copy.wait()


def opening(place, spectra, pick, put, keep, own, other, grown, devices):
    order = keep.shape[0]
    rows = order // devices
    width = own[0].shape[1] // 2
    last = spectra.shape[3]
    held = [own[0], other[0]]
    vmem = pl.BlockSpec(memory_space=pltpu.VMEM)
    return pl.pallas_call(
        functools.partial(opening_body, sources=len(held), scale=-1.0 / math.sqrt(order)),
        in_specs=[pl.BlockSpec(memory_space=pltpu.SMEM)]
        + [vmem] * 5
        + [pl.BlockSpec(memory_space=pl.ANY)] * len(held),
        out_specs=[pl.BlockSpec(memory_space=pl.ANY)] * 2,
        out_shape=[
            jax.ShapeDtypeStruct((devices, 2, rows, width), jnp.bfloat16),
            jax.ShapeDtypeStruct((order, 2 * last), jnp.bfloat16),
        ],
        scratch_shapes=[pltpu.VMEM(array.shape, jnp.bfloat16) for array in held]
        + [
            pltpu.VMEM((order, 2 * last), jnp.bfloat16),
            pltpu.VMEM((devices, 2, rows, width), jnp.bfloat16),
            pltpu.VMEM((order, 2 * width), jnp.bfloat16),
            pltpu.SemaphoreType.DMA((len(held),)),
            pltpu.SemaphoreType.DMA((1 + order // math.gcd(order, 256),)),
        ],
        compiler_params=pltpu.CompilerParams(vmem_limit_bytes=OPENING_VMEM),
        cost_estimate=pl.CostEstimate(
            flops=16 * order * order * width, bytes_accessed=8 * order * order, transcendentals=0
        ),
        name="opening",
    )(place, spectra, pick, put, keep, grown, *held)


def fill_tables(missing, neighbours, weights, order):
    shots = jnp.arange(order, dtype=jnp.int32)
    pick = jnp.zeros((missing.shape[0], order), jnp.float32)
    for slot in range(neighbours.shape[1]):
        pick = pick + jnp.where(
            neighbours[:, slot][:, None] == shots[None, :], weights[:, slot][:, None], 0.0
        )
    high = lax.reduce_precision(pick, 8, 7)
    found = shots[:, None] == missing[None, :]
    keep = 1.0 - jnp.any(found, axis=1, keepdims=True).astype(jnp.float32)
    both = jnp.concatenate([high, pick - high], axis=0).astype(jnp.bfloat16)
    return both, found.astype(jnp.bfloat16), keep


def spread(total, shares):
    widths = [total * share // PARTS for share in shares]
    return [(sum(widths[:index]), width) for index, width in enumerate(widths)]


def predict(records, missing, neighbours, weights, freq_bins):
    devices = lax.axis_size("shots")
    position = lax.axis_index("shots")
    shot_rows, order, samples = records.shape
    half = order // 2
    bins = freq_bins.shape[0]
    place_of = position.astype(jnp.int32).reshape(1)
    pairs = [(i, i ^ 1) for i in range(devices)]

    def exchange(blocks):
        return lax.all_to_all(blocks, "shots", split_axis=0, concat_axis=0, tiled=True)

    forward, inverse = tables(freq_bins, samples)
    pick, place, keep = fill_tables(missing, neighbours, weights, order)
    split = records.reshape(shot_rows, 2, half, samples)
    own, raw = [], []
    for first, width in spread(half, OUTWARD):
        block = forward_chunk(split, forward, first, width)
        block = exchange(block.reshape(devices, 2, shot_rows, width))
        raw.append(lax.ppermute(block, "shots", pairs))
        own.append(fill(block, pick, place, keep))
    grown = early(place_of, own[0], own[1])
    other = [fill(block, pick, place, keep) for block in raw[:-1]]
    mixed = devices <= LOOSE_DEVICES
    homeward = spread(half, HOMEWARD)
    result = None
    for index, (first, width) in enumerate(homeward):
        if index != 2:
            if index == 0:
                block, filled = opening(place_of, raw[-1], pick, place, keep, own, other, grown, devices)
                other = other + [filled]
            else:
                *blocks, final = closing(place_of, own, other, width, devices, mixed)
                block = blocks[0]
        else:
            block = final
        if index == 1 and mixed:
            arrived = [block]
            for step in range(1, devices):
                route = [(i, i ^ step) for i in range(devices)]
                arrived.append(lax.ppermute(blocks[step], "shots", route))
            result = loose_inverse(place_of, arrived, inverse, result, first)
        else:
            block = exchange(block)
            block = block.reshape(bins, 2, 2, shot_rows, width)
            result = inverse_chunk(block, inverse, result, first, half)
    return result.reshape(shot_rows, order, samples)


def solution(mesh):
    return jax.shard_map(
        predict,
        mesh=mesh,
        in_specs=(
            P(("lines", "shots"), None, None),
            P("lines"),
            P("lines", None),
            P("lines", None),
            P(),
        ),
        out_specs=P(("lines", "shots"), None, None),
        check_vma=False,
    )
```
